32 devices in a mesh: wide: 16 (over z, y, x), narrow: 2 (over core).
Axes of the slice: x: 2, y: 2, z: 4, core: 2. Of those that a mesh axis runs over, the one named last changes fastest.
Arguments:
- hidden_in: bfloat16 [4096, 4096], P('wide', 'narrow'), may hold values from -6 to 6
- norm_gain: bfloat16 [4096], P('narrow'), may hold values from 0.099609375 to 1.8984375
- w_query: bfloat16 [4096, 2048], P(None, 'narrow'), may hold values from -0.09375 to 0.09375
- key_weight: bfloat16 [4096, 512], P(None, 'narrow'), may hold values from -0.09375 to 0.09375
- value_weight: bfloat16 [4096, 512], P(None, 'narrow'), may hold values from -0.09375 to 0.09375
- w_out: bfloat16 [2048, 4096], P('narrow'), may hold values from -0.125 to 0.125
- cached_key_rows: bfloat16 [64, 512, 512], P('wide', None, 'narrow'), as said below
- cached_value_rows: bfloat16 [64, 512, 512], P('wide', None, 'narrow'), may hold values from -6 to 6
- lengths: int32 [64], P('wide'), may hold values from 32 to 512, as said below
- counts: int32 [64], P('wide'), may hold values from 32 to 64, as said below
- parents: int32 [64, 64], P('wide'), may hold values from 0 to 62, as said below
- accept: int32 [64, 8], P('wide'), may hold values from 0 to 21, as said below
- order_map: int32 [64], P('wide'), may hold values from 0 to 63, each once
- accept_head: bfloat16 [4096], P('narrow'), may hold values from -0.09375 to 0.09375
Outputs:
- hidden_out: bfloat16 [4096, 4096], P('wide', 'narrow')
- new_rows: bfloat16 [64, 8, 2, 512], P('wide', None, None, 'narrow')
- verify: float32 [64, 64], P('wide')
The draws below stay inside these ranges and needn't reach their ends.
Inputs may be any that keep to these rules, and one draw needn't show every extreme that they name: Request p's cache is live at positions below lengths[p]; positions beyond are padding. Request p uses slots 0 to counts[p] - 1; the other slots are padding. `parents`: slot 0 is the root and its own parent; the parent of slot i >= 1 is one of slots i - 3 to i - 1. `accept`: row p lists the first 8 slots of the path from slot 0 to some live slot of request p, root first. Initial request r is the request at position order_map[r] of every other request-indexed array. `cached_key_rows`: keys are stored already rotated to their positions.
All inputs are finite; a program needn't handle non-finite values.
Results may differ from the reference program's by a relative error of at most 0.012.
The reference program's roundings to bfloat16 on the way count: a program that leaves them out, or rounds other values in their place, can miss the bound.
Values may be sent and summed in bfloat16 or wider, within the bound.
A program may use at most 128 MiB of HBM per device.

```python
import math
import jax
import jax.numpy as jnp
from jax import lax

MODEL_WIDTH = 4096
QUERY_HEADS = 16
KEY_VALUE_HEADS = 4
HEAD_SIZE = 128
DRAFT_SLOTS = 64
ACC = 8
CACHE_SLOTS = 512
REQUEST_TOTAL = 64
TOKEN_TOTAL = 4096


def tree_parts(key):
    base = jax.random.fold_in(key, 7101)
    key_parent, key_count, key_full, key_target, key_least = jax.random.split(base, 5)
    slot_ids = jnp.arange(DRAFT_SLOTS, dtype=jnp.int32)
    lower = jnp.maximum(slot_ids - 3, 0)
    upper = jnp.maximum(slot_ids, 1)
    parents = jax.random.randint(key_parent, (REQUEST_TOTAL, DRAFT_SLOTS), lower[None, :], upper[None, :], dtype=jnp.int32)
    counts = jax.random.randint(key_count, (REQUEST_TOTAL,), DRAFT_SLOTS // 2, DRAFT_SLOTS + 1, dtype=jnp.int32)
    full_at = jax.random.randint(key_full, (), 0, REQUEST_TOTAL, dtype=jnp.int32)
    least_at = (full_at + jax.random.randint(key_least, (), 1, REQUEST_TOTAL, dtype=jnp.int32)) % REQUEST_TOTAL
    request_ids = jnp.arange(REQUEST_TOTAL, dtype=jnp.int32)
    counts = jnp.where(request_ids == full_at, DRAFT_SLOTS, counts)
    counts = jnp.where(request_ids == least_at, DRAFT_SLOTS // 2, counts)
    parents = jnp.where((request_ids == full_at)[:, None], lower[None, :], parents)
    target = jax.random.randint(key_target, (REQUEST_TOTAL,), 3 * ACC, counts, dtype=jnp.int32)
    target = jnp.where(request_ids == full_at, 3 * ACC, target)

    def climb(node, unused):
        upward = jnp.take_along_axis(parents, node[:, None], axis=1)[:, 0]
        return (upward, node)
    final_node, chain = lax.scan(climb, target, None, length=DRAFT_SLOTS)
    depth = jnp.sum((chain > 0).astype(jnp.int32), axis=0)
    picks = depth[None, :] - jnp.arange(ACC, dtype=jnp.int32)[:, None]
    accept = jnp.take_along_axis(chain, picks, axis=0).T
    return (parents, counts, accept)


def draw_parents(key, part):
    return tree_parts(key)[0]


def draw_counts(key, part):
    return tree_parts(key)[1]


def draw_accept(key, part):
    return tree_parts(key)[2]


def draw_lengths(key, part):
    base = jax.random.fold_in(key, 7202)
    key_len, key_full, key_least = jax.random.split(base, 3)
    lengths = jax.random.randint(key_len, (REQUEST_TOTAL,), CACHE_SLOTS // 16, CACHE_SLOTS + 1, dtype=jnp.int32)
    full_at = jax.random.randint(key_full, (), 0, REQUEST_TOTAL, dtype=jnp.int32)
    least_at = (full_at + jax.random.randint(key_least, (), 1, REQUEST_TOTAL, dtype=jnp.int32)) % REQUEST_TOTAL
    request_ids = jnp.arange(REQUEST_TOTAL, dtype=jnp.int32)
    lengths = jnp.where(request_ids == full_at, CACHE_SLOTS, lengths)
    return jnp.where(request_ids == least_at, CACHE_SLOTS // 16, lengths)


def draw_cached_key_rows(key, part):
    base = jax.random.fold_in(key, 7303)
    key_value_pair = jax.random.fold_in(base, 0)
    draft_values = jax.random.normal(key_value_pair, (REQUEST_TOTAL, CACHE_SLOTS, KEY_VALUE_HEADS * HEAD_SIZE), dtype=jnp.float32)
    return draft_values.astype(jnp.bfloat16)


def levels(rng, extent, shards, low, largest):
    gain = 1.0
    for axis_at, parts in shards:
        heights = jax.random.uniform(jax.random.fold_in(jax.random.fold_in(rng, 6), axis_at), (parts,), jnp.float32, low / len(shards), largest / len(shards))
        gain = gain * jnp.repeat(jnp.exp(heights), extent[axis_at] // parts).reshape((-1,) + (1,) * (len(extent) - 1 - axis_at))
    return gain


def bell_draw(stream_key, shape, scale, reach, cuts=(), kind=jnp.bfloat16):
    values = jax.random.normal(stream_key, shape, jnp.float32) * scale
    if len(cuts) > 0:
        values = levels(stream_key, shape, cuts, -0.22, 0.18) * values
    return jnp.clip(values, min=-reach, max=reach).astype(kind)


def setup_inputs(seed: int = 0) -> dict:
    key_of = jax.random.split(jax.random.key(seed), 15)
    hidden_in = bell_draw(key_of[0], (TOKEN_TOTAL, MODEL_WIDTH), 1.0, 6.0, ((0, 16), (1, 2)))
    norm_gain = jnp.clip(1.0 + 0.18 * jax.random.normal(key_of[1], (MODEL_WIDTH,), jnp.float32), 0.099609375, 1.8984375).astype(jnp.bfloat16)
    w_query = bell_draw(key_of[2], (MODEL_WIDTH, QUERY_HEADS * HEAD_SIZE), MODEL_WIDTH ** -0.5, 0.09375, ((1, 2),))
    key_weight = bell_draw(key_of[3], (MODEL_WIDTH, KEY_VALUE_HEADS * HEAD_SIZE), MODEL_WIDTH ** -0.5, 0.09375, ((1, 2),))
    value_weight = bell_draw(key_of[4], (MODEL_WIDTH, KEY_VALUE_HEADS * HEAD_SIZE), MODEL_WIDTH ** -0.5, 0.09375, ((1, 2),))
    w_out = bell_draw(key_of[5], (QUERY_HEADS * HEAD_SIZE, MODEL_WIDTH), (QUERY_HEADS * HEAD_SIZE) ** -0.5, 0.125, ((0, 2),))
    cached_key_rows = draw_cached_key_rows(jax.random.fold_in(key_of[14], 71), 0)
    cached_value_rows = bell_draw(key_of[7], (REQUEST_TOTAL, CACHE_SLOTS, KEY_VALUE_HEADS * HEAD_SIZE), 1.0, 6.0, ((0, 16), (2, 2)))
    lengths = draw_lengths(jax.random.fold_in(key_of[14], 71), 0)
    counts = draw_counts(jax.random.fold_in(key_of[14], 71), 0)
    parents = draw_parents(jax.random.fold_in(key_of[14], 71), 0)
    accept = draw_accept(jax.random.fold_in(key_of[14], 71), 0)
    order_map = jax.random.permutation(key_of[12], REQUEST_TOTAL).astype(jnp.int32)
    accept_head = bell_draw(key_of[13], (MODEL_WIDTH,), MODEL_WIDTH ** -0.5, 0.09375, ((0, 2),))
    return dict(hidden_in=hidden_in, norm_gain=norm_gain, w_query=w_query, key_weight=key_weight, value_weight=value_weight, w_out=w_out, cached_key_rows=cached_key_rows, cached_value_rows=cached_value_rows, lengths=lengths, counts=counts, parents=parents, accept=accept, order_map=order_map, accept_head=accept_head)


masked_score = -1e+30
rms_epsilon = 1e-05

def ancestry_of(parents):
    slot_ids = jnp.arange(parents.shape[-1], dtype=jnp.int32)
    linked = ((slot_ids[None, None, :] == parents[:, :, None]) | (slot_ids[None, :, None] == slot_ids[None, None, :])).astype(jnp.float32)
    for doubling in range(max(1, (parents.shape[-1] - 1).bit_length())):
        linked = jnp.minimum(jnp.einsum('rij,rjk->rik', linked, linked, precision=lax.Precision.HIGHEST), 1.0)
    return linked

def apply_rotary(draft_values, token_positions):
    head_dim = draft_values.shape[-1]
    half_dim = head_dim // 2
    freqs = 10000.0 ** (-(jnp.arange(half_dim, dtype=jnp.float32) * 2.0 / head_dim))
    angles = token_positions[:, None] * freqs[None, :]
    cosine = jnp.cos(angles)[:, None, :]
    sine = jnp.sin(angles)[:, None, :]
    first = draft_values[..., :half_dim]
    second = draft_values[..., half_dim:]
    return jnp.concatenate([first * cosine - second * sine, second * cosine + first * sine], axis=-1)

def attend_layer(request_items):
    query_part, keys_part, values_part, cache_k, cache_v, length, count, ancestor_mask = request_items
    draft_len, head_count, head_dim = query_part.shape
    kv_heads = keys_part.shape[1]
    group_size = head_count // kv_heads
    cache_len = cache_k.shape[0]
    score_scale = 1.0 / math.sqrt(head_dim)
    queries = query_part.reshape(draft_len, kv_heads, group_size, head_dim).transpose(1, 2, 0, 3).reshape(kv_heads, group_size * draft_len, head_dim).astype(jnp.float32)
    keys_cache = cache_k.reshape(cache_len, kv_heads, head_dim).astype(jnp.float32)
    values_cache = cache_v.reshape(cache_len, kv_heads, head_dim).astype(jnp.float32)
    slot_ids = jnp.arange(draft_len, dtype=jnp.int32)
    allowed = jnp.tile((ancestor_mask > 0.5) & (slot_ids[None, :] < count), (group_size, 1))[None]
    live_mask = (jnp.arange(cache_len, dtype=jnp.int32) < length)[None, None, :]
    score_cache = jnp.einsum('grd,kgd->grk', queries, keys_cache) * score_scale
    score_cache = jnp.where(live_mask, score_cache, masked_score)
    score_draft = jnp.einsum('grd,jgd->grj', queries, keys_part.astype(jnp.float32)) * score_scale
    score_draft = jnp.where(allowed, score_draft, masked_score)
    highest = jnp.maximum(lax.optimization_barrier(jnp.max(score_cache, axis=-1)), lax.optimization_barrier(jnp.max(score_draft, axis=-1)))[..., None]
    probs_cache = jnp.where(live_mask, jnp.exp(score_cache - highest), 0.0)
    probs_draft = jnp.where(allowed, jnp.exp(score_draft - highest), 0.0)
    total = lax.optimization_barrier(jnp.sum(probs_cache, axis=-1)) + lax.optimization_barrier(jnp.sum(probs_draft, axis=-1))
    rounded_cache = lax.optimization_barrier(probs_cache.astype(jnp.bfloat16)).astype(jnp.float32)
    rounded_draft = lax.optimization_barrier(probs_draft.astype(jnp.bfloat16)).astype(jnp.float32)
    weighted = jnp.einsum('grk,kgd->grd', rounded_cache, values_cache) + jnp.einsum('grj,jgd->grd', rounded_draft, values_part.astype(jnp.float32))
    result = (weighted / total[..., None]).astype(jnp.bfloat16)
    return result.reshape(kv_heads, group_size, draft_len, head_dim).transpose(2, 0, 1, 3).reshape(draft_len, head_count * head_dim)

def reference(hidden_in, norm_gain, w_query, key_weight, value_weight, w_out, cached_key_rows, cached_value_rows, lengths, counts, parents, accept, order_map, accept_head):
    inputs = hidden_in.astype(jnp.float32)
    mean_square = lax.optimization_barrier(jnp.mean(inputs * inputs, axis=1, keepdims=True))
    normed = (inputs * lax.rsqrt(mean_square + rms_epsilon) * norm_gain.astype(jnp.float32)).astype(jnp.bfloat16)
    query = jnp.dot(normed, w_query, preferred_element_type=jnp.float32)
    draft_keys = jnp.dot(normed, key_weight, preferred_element_type=jnp.float32)
    value = jnp.dot(normed, value_weight, preferred_element_type=jnp.float32)
    ancestor_mask = ancestry_of(parents)
    depth = lax.optimization_barrier(jnp.sum(ancestor_mask, axis=-1)) - 1.0
    token_positions = (lengths[:, None].astype(jnp.float32) + depth).reshape(TOKEN_TOTAL)
    rotated_query = lax.optimization_barrier(apply_rotary(query.reshape(TOKEN_TOTAL, QUERY_HEADS, HEAD_SIZE), token_positions).astype(jnp.bfloat16))
    rotated_keys = lax.optimization_barrier(apply_rotary(draft_keys.reshape(TOKEN_TOTAL, KEY_VALUE_HEADS, HEAD_SIZE), token_positions).astype(jnp.bfloat16))
    fresh_values = lax.optimization_barrier(value.astype(jnp.bfloat16))
    attended_rows = lax.map(attend_layer, (rotated_query.reshape(REQUEST_TOTAL, DRAFT_SLOTS, QUERY_HEADS, HEAD_SIZE), rotated_keys.reshape(REQUEST_TOTAL, DRAFT_SLOTS, KEY_VALUE_HEADS, HEAD_SIZE), fresh_values.reshape(REQUEST_TOTAL, DRAFT_SLOTS, KEY_VALUE_HEADS, HEAD_SIZE), cached_key_rows, cached_value_rows, lengths, counts, ancestor_mask))
    attended_rows = attended_rows.reshape(TOKEN_TOTAL, QUERY_HEADS * HEAD_SIZE)
    mixed = jnp.dot(attended_rows, w_out, preferred_element_type=jnp.float32)
    live_rows = (jnp.arange(DRAFT_SLOTS, dtype=jnp.int32)[None, :] < counts[:, None]).reshape(TOKEN_TOTAL)
    hidden_out = jnp.where(live_rows[:, None], inputs + mixed, 0.0).astype(jnp.bfloat16)
    key_matrix = jnp.take_along_axis(rotated_keys.reshape(REQUEST_TOTAL, DRAFT_SLOTS, KEY_VALUE_HEADS * HEAD_SIZE), accept[:, :, None], axis=1)
    value_matrix = jnp.take_along_axis(fresh_values.reshape(REQUEST_TOTAL, DRAFT_SLOTS, KEY_VALUE_HEADS * HEAD_SIZE), accept[:, :, None], axis=1)
    new_rows = jnp.stack([key_matrix, value_matrix], axis=2)
    processed = lax.optimization_barrier(jnp.sum(hidden_out.astype(jnp.float32) * accept_head.astype(jnp.float32)[None, :], axis=1)).reshape(REQUEST_TOTAL, DRAFT_SLOTS)
    verify = jnp.take(processed, order_map, axis=0)
    return (hidden_out, new_rows, verify)
```

```python
import functools
import math

import jax
import jax.numpy as jnp
import numpy as np
from jax import lax
from jax.experimental import pallas as pl
from jax.experimental.pallas import tpu as pltpu
from jax.sharding import PartitionSpec as P

HEAD_SIZE = 128
MESH = pl.DeviceIdType.MESH
Q_COLS = 256
O_COLS = 512

masked_score = -1e30
rms_epsilon = 1e-05


def finish_kernel(
    hidden_ref, rows_ref, scores_ref, out_ref, new_rows_ref, verify_ref, out_sems
):
    pieces = out_sems.shape[0]
    stores = [
        pltpu.make_async_copy(
            hidden_ref.at[n], out_ref.at[:, pl.ds(n * O_COLS, O_COLS)], out_sems.at[n]
        )
        for n in range(pieces)
    ]
    for store in stores:
        store.start()
    new_rows_ref[...] = rows_ref[...].astype(jnp.float32).reshape(new_rows_ref.shape).astype(
        new_rows_ref.dtype
    )
    verify_ref[...] = scores_ref[...]
    for store in stores:
        store.wait()


def layer_kernel(
    wide_count,
    narrow_count,
    hidden_hbm,
    gain_ref,
    head_ref,
    freqs_ref,
    wq_hbm,
    wk_hbm,
    wv_hbm,
    wo_hbm,
    ck_hbm,
    cv_hbm,
    parents_ref,
    lengths_ref,
    counts_ref,
    accept_ref,
    order_ref,
    out_ref,
    rows_ref,
    verify_ref,
    hid,
    normed,
    squares,
    wq,
    wk,
    wv,
    wo,
    ck,
    cv,
    projected,
    anc,
    cosine,
    sine,
    live,
    q_rot,
    k_rot,
    v_new,
    att,
    part_send,
    part_recv,
    score_acc,
    mine,
    gathered,
    load_sems,
    wo_sems,
    square_sems,
    norm_send,
    norm_recv,
    part_send_sems,
    part_recv_sems,
    all_send,
    all_recv,
):
    me_wide = lax.axis_index("wide")
    me = lax.axis_index("narrow")
    other = 1 - me
    device_count = wide_count * narrow_count
    flat = me_wide * narrow_count + me
    rows, half = hid.shape
    requests, slots = parents_ref.shape
    q_width = wq_hbm.shape[1]
    half_chunks = half // O_COLS
    key_heads = wk_hbm.shape[1] // HEAD_SIZE
    group = q_width // HEAD_SIZE // key_heads
    cache_len = ck.shape[1]
    partner = (me_wide, other)
    norm_blocks = norm_send.shape[0]
    norm_rows = rows // norm_blocks

    def target_of(step):
        target = lax.rem(flat + 1 + step, device_count)
        return (target // narrow_count, lax.rem(target, narrow_count))

    barrier = pltpu.get_barrier_semaphore()
    load_hid = pltpu.make_async_copy(hidden_hbm, hid, load_sems.at[0])
    load_hid.start()
    loads = []
    for part, owner in enumerate((me, other)):
        from_rows = pl.ds(pl.multiple_of(owner * half, half), half)
        for at, (hbm, vmem) in enumerate(((wq_hbm, wq), (wk_hbm, wk), (wv_hbm, wv))):
            loads.append(
                pltpu.make_async_copy(
                    hbm.at[from_rows, :], vmem.at[part], load_sems.at[1 + 3 * part + at]
                )
            )
    for load in loads[:3]:
        load.start()

    @pl.loop(0, device_count - 1)
    def _(step):
        pl.semaphore_signal(
            barrier, inc=1, device_id=target_of(step), device_id_type=MESH
        )

    for load in loads[3:]:
        load.start()
    load_ck = pltpu.make_async_copy(ck_hbm, ck, load_sems.at[7])
    load_cv = pltpu.make_async_copy(cv_hbm, cv, load_sems.at[8])
    load_ck.start()
    load_cv.start()

    def wo_load(at):
        side = other if at < half_chunks else me
        column = side * half + at % half_chunks * O_COLS
        return pltpu.make_async_copy(
            wo_hbm.at[:, pl.ds(pl.multiple_of(column, O_COLS), O_COLS)],
            wo.at[at],
            wo_sems.at[at],
        )

    for at in range(2 * half_chunks):
        wo_load(at).start()

    lane64 = lax.broadcasted_iota(jnp.int32, (slots, slots), 1)
    eye64 = lax.broadcasted_iota(jnp.int32, (slots, slots), 0) == lane64
    parent_columns = []
    for p in range(requests):
        row = jnp.broadcast_to(parents_ref[p : p + 1, :].astype(jnp.float32), (slots, slots))
        parent_columns.append(
            jnp.sum(jnp.where(eye64, row, 0.0), axis=1, keepdims=True) + float(p * slots)
        )
    parent_column = jnp.concatenate(parent_columns, axis=0).astype(jnp.int32)
    row_at = lax.broadcasted_iota(jnp.int32, (rows, rows), 0)
    lane_at = lax.broadcasted_iota(jnp.int32, (rows, rows), 1)
    linked = jnp.where((lane_at == parent_column) | (row_at == lane_at), 1.0, 0.0).astype(
        jnp.bfloat16
    )
    for doubling in range(max(1, (slots - 1).bit_length())):
        linked = jnp.minimum(
            jnp.dot(linked, linked, preferred_element_type=jnp.float32), 1.0
        ).astype(jnp.bfloat16)

    load_hid.wait()
    step_rows = 16

    @pl.loop(0, rows // step_rows)
    def _(block):
        at = pl.ds(pl.multiple_of(block * step_rows, step_rows), step_rows)
        total = jnp.zeros((step_rows, HEAD_SIZE), jnp.float32)
        for tile in range(half // HEAD_SIZE):
            piece = hid[at, tile * HEAD_SIZE : (tile + 1) * HEAD_SIZE].astype(jnp.float32)
            total = total + piece * piece
        squares[0, at, :] = total

    pl.semaphore_wait(barrier, device_count - 1)
    square_copy = pltpu.make_async_remote_copy(
        src_ref=squares.at[0],
        dst_ref=squares.at[1],
        send_sem=square_sems.at[0],
        recv_sem=square_sems.at[1],
        device_id=partner,
        device_id_type=MESH,
    )
    square_copy.start()

    depth = jnp.sum(linked.astype(jnp.float32), axis=1, keepdims=True) - 1.0
    fold_row = lax.broadcasted_iota(jnp.int32, (rows, slots), 0)
    fold_lane = lax.broadcasted_iota(jnp.int32, (rows, slots), 1)
    fold = jnp.where(lax.rem(fold_row, slots) == fold_lane, 1.0, 0.0).astype(jnp.bfloat16)
    anc[...] = jnp.dot(linked, fold, preferred_element_type=jnp.float32)
    row_id = lax.broadcasted_iota(jnp.int32, (rows, HEAD_SIZE), 0)
    lane_id = lax.broadcasted_iota(jnp.int32, (rows, HEAD_SIZE), 1)
    length_at = jnp.zeros((rows, HEAD_SIZE), jnp.float32)
    end_at = jnp.zeros((rows, HEAD_SIZE), jnp.int32)
    for p in range(requests):
        here = row_id // slots == p
        length_at = jnp.where(here, lengths_ref[p].astype(jnp.float32), length_at)
        end_at = jnp.where(here, counts_ref[p] + p * slots, end_at)
    live[...] = jnp.where(row_id < end_at, 1.0, 0.0)
    angles = (length_at + depth) * freqs_ref[...]
    cosine[...] = jnp.cos(angles)
    turned = jnp.sin(angles)
    sine[...] = jnp.where(lane_id < HEAD_SIZE // 2, -turned, turned)
    gain = gain_ref[...].astype(jnp.float32).reshape(1, half)

    square_copy.wait()

    def norm_copy(block):
        at = pl.ds(block * norm_rows, norm_rows)
        return pltpu.make_async_remote_copy(
            src_ref=normed.at[0, at, :],
            dst_ref=normed.at[1, at, :],
            send_sem=norm_send.at[block],
            recv_sem=norm_recv.at[block],
            device_id=partner,
            device_id_type=MESH,
        )

    for block in range(norm_blocks):
        for first in range(block * norm_rows, (block + 1) * norm_rows, step_rows):
            at = slice(first, first + step_rows)
            square = jnp.sum(squares[0, at, :] + squares[1, at, :], axis=1, keepdims=True)
            scale = lax.rsqrt(square / (2.0 * half) + rms_epsilon)
            normed[0, at, :] = (hid[at, :].astype(jnp.float32) * scale * gain).astype(
                jnp.bfloat16
            )
        norm_copy(block).start()

    def rotate(block):
        return (block * cosine[...] + pltpu.roll(block, HEAD_SIZE // 2, 1) * sine[...]).astype(
            jnp.bfloat16
        )

    def weight(part, n):
        if n < q_width // Q_COLS:
            return wq[part, :, n * Q_COLS : (n + 1) * Q_COLS]
        return (wk if n == q_width // Q_COLS else wv)[part]

    chunks = q_width // Q_COLS + 2
    for n in range(chunks):
        if n == 0:
            loads[0].wait()
        if n >= chunks - 2:
            loads[n - chunks + 3].wait()
        projected[n] = jnp.dot(normed[0], weight(0, n), preferred_element_type=jnp.float32)
    for block in range(norm_blocks):
        norm_copy(block).wait()
    for n in range(chunks):
        if n == 0:
            loads[3].wait()
        if n >= chunks - 2:
            loads[n - chunks + 6].wait()
        product = projected[n] + jnp.dot(
            normed[1], weight(1, n), preferred_element_type=jnp.float32
        )
        if n == chunks - 1:
            v_new[...] = product.astype(jnp.bfloat16)
            continue
        for h in range(product.shape[1] // HEAD_SIZE):
            turned = rotate(product[:, h * HEAD_SIZE : (h + 1) * HEAD_SIZE])
            if n == chunks - 2:
                k_rot[:, h * HEAD_SIZE : (h + 1) * HEAD_SIZE] = turned
            else:
                first = n * Q_COLS + h * HEAD_SIZE
                q_rot[:, first : first + HEAD_SIZE] = turned

    load_ck.wait()
    load_cv.wait()
    factor = math.log2(math.e) / math.sqrt(HEAD_SIZE)
    contract_last = (((1,), (1,)), ((), ()))
    cache_lane = lax.broadcasted_iota(jnp.int32, (group * slots, cache_len), 1)
    slot_lane = lax.broadcasted_iota(jnp.int32, (slots, slots), 1)

    @pl.loop(0, requests, unroll=True)
    def _(p):
        at = pl.ds(pl.multiple_of(p * slots, slots), slots)
        allowed = jnp.where(slot_lane < counts_ref[p], anc[at, :], 0.0)
        allowed = jnp.concatenate([allowed] * group, axis=0) > 0.5
        alive = cache_lane < lengths_ref[p]
        for g in range(key_heads):
            columns = slice(g * HEAD_SIZE, (g + 1) * HEAD_SIZE)
            pieces = []
            for h in range(group):
                head = g * group + h
                pieces.append(q_rot[at, head * HEAD_SIZE : (head + 1) * HEAD_SIZE])
            queries = jnp.concatenate(pieces, axis=0)
            cached = jnp.where(
                alive,
                lax.dot_general(
                    queries, ck[p, :, columns], contract_last, preferred_element_type=jnp.float32
                ),
                masked_score,
            )
            fresh = jnp.where(
                allowed,
                lax.dot_general(
                    queries, k_rot[at, columns], contract_last, preferred_element_type=jnp.float32
                ),
                masked_score,
            )
            highest = jnp.maximum(
                jnp.max(cached, axis=1, keepdims=True), jnp.max(fresh, axis=1, keepdims=True)
            )
            cached = jnp.exp2((cached - highest) * factor)
            fresh = jnp.exp2((fresh - highest) * factor)
            total = jnp.sum(cached, axis=1, keepdims=True) + jnp.sum(
                fresh, axis=1, keepdims=True
            )
            weighted = jnp.dot(
                cached.astype(jnp.bfloat16), cv[p, :, columns], preferred_element_type=jnp.float32
            ) + jnp.dot(
                fresh.astype(jnp.bfloat16), v_new[at, columns], preferred_element_type=jnp.float32
            )
            result = (weighted / total).astype(jnp.bfloat16)
            for h in range(group):
                head = g * group + h
                att[at, head * HEAD_SIZE : (head + 1) * HEAD_SIZE] = result[
                    h * slots : (h + 1) * slots
                ]

    def part_copy(c):
        return pltpu.make_async_remote_copy(
            src_ref=part_send.at[c],
            dst_ref=part_recv.at[c],
            send_sem=part_send_sems.at[c],
            recv_sem=part_recv_sems.at[c],
            device_id=partner,
            device_id_type=MESH,
        )

    for c in range(half_chunks):
        wo_load(c).wait()
        part_send[c] = jnp.dot(att[...], wo[c], preferred_element_type=jnp.float32).astype(
            jnp.bfloat16
        )
        part_copy(c).start()

    for c in range(half_chunks):
        wo_load(half_chunks + c).wait()
        own = jnp.dot(att[...], wo[half_chunks + c], preferred_element_type=jnp.float32)
        part_copy(c).wait()
        at = slice(c * O_COLS, (c + 1) * O_COLS)
        summed = hid[:, at].astype(jnp.float32) + own + part_recv[c].astype(jnp.float32)
        head = head_ref[at].astype(jnp.float32).reshape(1, O_COLS)
        scored = jnp.zeros((rows, HEAD_SIZE), jnp.float32)
        for part in range(O_COLS // HEAD_SIZE):
            columns = slice(part * HEAD_SIZE, (part + 1) * HEAD_SIZE)
            kept = jnp.where(live[...] > 0.5, summed[:, columns], 0.0).astype(jnp.bfloat16)
            out_ref[c, :, columns] = kept
            scored = scored + kept.astype(jnp.float32) * head[:, columns]
        score_acc[...] = scored if c == 0 else score_acc[...] + scored

    per_line = HEAD_SIZE // slots
    line_row = lax.broadcasted_iota(jnp.int32, (slots, HEAD_SIZE), 0)
    line_lane = lax.broadcasted_iota(jnp.int32, (slots, HEAD_SIZE), 1)
    lines = []
    for first in range(0, requests, per_line):
        line = jnp.zeros((slots, HEAD_SIZE), jnp.float32)
        for p in range(first, first + per_line):
            column = jnp.sum(score_acc[p * slots : (p + 1) * slots, :], axis=1, keepdims=True)
            line = jnp.where(line_lane - (p - first) * slots == line_row, column, line)
        lines.append(jnp.sum(line, axis=0, keepdims=True))
    scores = jnp.concatenate(lines, axis=0)
    mine[...] = scores
    gathered[flat] = scores

    @pl.loop(0, device_count - 1)
    def _(step):
        pltpu.make_async_remote_copy(
            src_ref=mine,
            dst_ref=gathered.at[flat],
            send_sem=all_send,
            recv_sem=all_recv,
            device_id=target_of(step),
            device_id_type=MESH,
        ).start()

    picks = rows_ref.shape[0]
    per_request = picks // requests // 2
    pick_row = lax.broadcasted_iota(jnp.int32, (picks, rows), 0)
    pick_lane = lax.broadcasted_iota(jnp.int32, (picks, rows), 1)
    wanted = jnp.zeros((picks, rows), jnp.int32)
    for p in range(requests):
        for a in range(per_request):
            wanted = jnp.where(
                pick_row // 2 == p * per_request + a, accept_ref[p, a] + p * slots, wanted
            )
    chosen = pick_lane == wanted
    odd = lax.rem(pick_row, 2) == 1
    pick_keys = jnp.where(chosen & ~odd, 1.0, 0.0).astype(jnp.bfloat16)
    pick_values = jnp.where(chosen & odd, 1.0, 0.0).astype(jnp.bfloat16)
    rows_ref[...] = (
        jnp.dot(pick_keys, k_rot[...], preferred_element_type=jnp.float32)
        + jnp.dot(pick_values, v_new[...], preferred_element_type=jnp.float32)
    ).astype(jnp.bfloat16)

    everything = gathered.at[pl.ds(0, device_count - 1)]
    whole = pltpu.make_async_remote_copy(
        src_ref=everything,
        dst_ref=everything,
        send_sem=all_send,
        recv_sem=all_recv,
        device_id=partner,
        device_id_type=MESH,
    )
    whole.wait_send()
    whole.wait_recv()

    shape = (device_count, requests // per_line, HEAD_SIZE)
    source = lax.broadcasted_iota(jnp.int32, shape, 0) // narrow_count
    line_at = lax.broadcasted_iota(jnp.int32, shape, 1)
    place = lax.broadcasted_iota(jnp.int32, shape, 2) // slots
    request_at = source * requests + line_at * per_line + place
    values = gathered[...]
    for r in range(requests):
        picked = jnp.sum(jnp.where(request_at == order_ref[r], values, 0.0), axis=0)
        picked = jnp.sum(picked, axis=0, keepdims=True)
        total = picked[:, :slots]
        for part in range(1, per_line):
            total = total + picked[:, part * slots : (part + 1) * slots]
        verify_ref[r : r + 1, :] = total


def body(
    hidden_in,
    norm_gain,
    w_query,
    key_weight,
    value_weight,
    w_out,
    cached_key_rows,
    cached_value_rows,
    lengths,
    counts,
    parents,
    accept,
    order_map,
    accept_head,
):
    wide_count = lax.axis_size("wide")
    narrow_count = lax.axis_size("narrow")
    device_count = wide_count * narrow_count
    rows, half = hidden_in.shape
    requests, slots = parents.shape
    per_request = accept.shape[1]
    query_width = w_query.shape[1]
    key_width = key_weight.shape[1]
    norm_blocks = 4
    half_chunks = half // O_COLS
    q_chunks = query_width // Q_COLS
    exponents = np.arange(HEAD_SIZE) % (HEAD_SIZE // 2) * 2.0 / HEAD_SIZE
    freqs = jnp.asarray((10000.0**-exponents)[None, :].astype(np.float32))
    hbm_spec = pl.BlockSpec(memory_space=pltpu.HBM)
    vmem_spec = pl.BlockSpec(memory_space=pltpu.VMEM)
    smem_spec = pl.BlockSpec(memory_space=pltpu.SMEM)
    bf16, f32 = jnp.bfloat16, jnp.float32
    hidden, picked_rows, scores = pl.pallas_call(
        functools.partial(layer_kernel, wide_count, narrow_count),
        out_shape=(
            jax.ShapeDtypeStruct((half_chunks, rows, O_COLS), bf16),
            jax.ShapeDtypeStruct((requests * per_request * 2, key_width), bf16),
            jax.ShapeDtypeStruct((requests, slots), f32),
        ),
        in_specs=[hbm_spec, vmem_spec, vmem_spec, vmem_spec]
        + [hbm_spec] * 6
        + [vmem_spec]
        + [smem_spec] * 4,
        out_specs=(vmem_spec, vmem_spec, vmem_spec),
        scratch_shapes=[
            pltpu.VMEM((rows, half), bf16),
            pltpu.VMEM((2, rows, half), bf16),
            pltpu.VMEM((2, rows, HEAD_SIZE), f32),
            pltpu.VMEM((2, half, query_width), bf16),
            pltpu.VMEM((2, half, key_width), bf16),
            pltpu.VMEM((2, half, key_width), bf16),
            pltpu.VMEM((2 * half_chunks, query_width, O_COLS), bf16),
            pltpu.VMEM(cached_key_rows.shape, bf16),
            pltpu.VMEM(cached_value_rows.shape, bf16),
            pltpu.VMEM((q_chunks + 2, rows, Q_COLS), f32),
            pltpu.VMEM((rows, slots), f32),
            pltpu.VMEM((rows, HEAD_SIZE), f32),
            pltpu.VMEM((rows, HEAD_SIZE), f32),
            pltpu.VMEM((rows, HEAD_SIZE), f32),
            pltpu.VMEM((rows, query_width), bf16),
            pltpu.VMEM((rows, key_width), bf16),
            pltpu.VMEM((rows, key_width), bf16),
            pltpu.VMEM((rows, query_width), bf16),
            pltpu.VMEM((half_chunks, rows, O_COLS), bf16),
            pltpu.VMEM((half_chunks, rows, O_COLS), bf16),
            pltpu.VMEM((rows, HEAD_SIZE), f32),
            pltpu.VMEM((requests * slots // HEAD_SIZE, HEAD_SIZE), f32),
            pltpu.VMEM((device_count, requests * slots // HEAD_SIZE, HEAD_SIZE), f32),
            pltpu.SemaphoreType.DMA((9,)),
            pltpu.SemaphoreType.DMA((2 * half_chunks,)),
            pltpu.SemaphoreType.DMA((2,)),
            pltpu.SemaphoreType.DMA((norm_blocks,)),
            pltpu.SemaphoreType.DMA((norm_blocks,)),
            pltpu.SemaphoreType.DMA((half_chunks,)),
            pltpu.SemaphoreType.DMA((half_chunks,)),
            pltpu.SemaphoreType.DMA,
            pltpu.SemaphoreType.DMA,
        ],
        compiler_params=pltpu.CompilerParams(
            collective_id=0, has_side_effects=True, vmem_limit_bytes=48 * 2**20
        ),
    )(
        *(
            pltpu.with_memory_space_constraint(operand, pltpu.HBM)
            for operand in (
                hidden_in,
                norm_gain,
                accept_head,
                freqs,
                w_query,
                key_weight,
                value_weight,
                w_out,
                cached_key_rows,
                cached_value_rows,
                parents,
                lengths,
                counts,
                accept,
                order_map,
            )
        )
    )
    return pl.pallas_call(
        finish_kernel,
        out_shape=(
            jax.ShapeDtypeStruct((rows, half), bf16),
            jax.ShapeDtypeStruct((requests, per_request, 2, key_width), bf16),
            jax.ShapeDtypeStruct((requests, slots), f32),
        ),
        in_specs=[vmem_spec, vmem_spec, vmem_spec],
        out_specs=(hbm_spec, vmem_spec, vmem_spec),
        scratch_shapes=[pltpu.SemaphoreType.DMA((half_chunks,))],
        compiler_params=pltpu.CompilerParams(vmem_limit_bytes=8 * 2**20),
    )(hidden, picked_rows, scores)


def solution(mesh):
    placed = (
        P("wide", "narrow"),
        P("narrow"),
        P(None, "narrow"),
        P(None, "narrow"),
        P(None, "narrow"),
        P("narrow", None),
        P("wide", None, "narrow"),
        P("wide", None, "narrow"),
        P("wide"),
        P("wide"),
        P("wide", None),
        P("wide", None),
        P("wide"),
        P("narrow"),
    )
    return jax.shard_map(
        body,
        mesh=mesh,
        in_specs=placed,
        out_specs=(P("wide", "narrow"), P("wide", None, None, "narrow"), P("wide", None)),
        check_vma=False,
    )
```

```python
import functools
import math

import jax
import jax.numpy as jnp
import numpy as np
from jax import lax
from jax.experimental import pallas as pl
from jax.experimental.pallas import tpu as pltpu
from jax.sharding import PartitionSpec as P

HEAD_SIZE = 128
MESH = pl.DeviceIdType.MESH
Q_COLS = 256
O_COLS = 512

masked_score = -1e30
rms_epsilon = 1e-05


def finish_kernel(
    hidden_ref, rows_ref, scores_ref, out_ref, new_rows_ref, verify_ref, out_sems
):
    pieces = hidden_ref.shape[0]
    stores = [
        pltpu.make_async_copy(
            hidden_ref.at[n], out_ref.at[:, pl.ds(n * O_COLS, O_COLS)], out_sems.at[n]
        )
        for n in range(pieces)
    ]
    stores.append(pltpu.make_async_copy(rows_ref, new_rows_ref, out_sems.at[pieces]))
    stores.append(pltpu.make_async_copy(scores_ref, verify_ref, out_sems.at[pieces + 1]))
    for store in stores:
        store.start()
    for store in stores:
        store.wait()


def layer_kernel(
    wide_count,
    narrow_count,
    hidden_hbm,
    gain_hbm,
    head_hbm,
    freqs_hbm,
    wq_hbm,
    wk_hbm,
    wv_hbm,
    wo_hbm,
    ck_hbm,
    cv_hbm,
    parents_hbm,
    lengths_hbm,
    counts_hbm,
    accept_hbm,
    order_hbm,
    out_ref,
    rows_ref,
    verify_ref,
    gain_ref,
    head_ref,
    freqs_ref,
    parents_ref,
    lengths_ref,
    counts_ref,
    accept_ref,
    order_ref,
    hid,
    normed,
    squares,
    wq,
    wk,
    wv,
    wo,
    ck,
    cv,
    projected,
    own_part,
    anc,
    cosine,
    sine,
    live,
    q_rot,
    k_rot,
    v_new,
    att,
    part_send,
    part_recv,
    score_acc,
    mine,
    gathered,
    small_sems,
    load_sems,
    wo_sems,
    square_sems,
    norm_send,
    norm_recv,
    part_send_sems,
    part_recv_sems,
    all_send,
    all_recv,
):
    me_wide = lax.axis_index("wide")
    me = lax.axis_index("narrow")
    other = 1 - me
    device_count = wide_count * narrow_count
    flat = me_wide * narrow_count + me
    rows, half = hid.shape
    requests, slots = parents_ref.shape
    q_width = wq_hbm.shape[1]
    half_chunks = half // O_COLS
    key_heads = wk_hbm.shape[1] // HEAD_SIZE
    group = q_width // HEAD_SIZE // key_heads
    cache_len = ck.shape[1]
    partner = (me_wide, other)
    norm_blocks = norm_send.shape[0]
    norm_rows = rows // norm_blocks
    mid = rows // 2
    sides = (slice(0, mid), slice(mid, rows))

    def target_of(step):
        target = lax.rem(flat + 1 + step, device_count)
        return (target // narrow_count, lax.rem(target, narrow_count))

    barrier = pltpu.get_barrier_semaphore()
    load_hid = pltpu.make_async_copy(hidden_hbm, hid, load_sems.at[0])
    load_hid.start()
    small = [
        pltpu.make_async_copy(hbm, there, small_sems.at[at])
        for at, (hbm, there) in enumerate(
            (
                (parents_hbm, parents_ref),
                (gain_hbm, gain_ref),
                (freqs_hbm, freqs_ref),
                (head_hbm, head_ref),
                (lengths_hbm, lengths_ref),
                (counts_hbm, counts_ref),
                (accept_hbm, accept_ref),
                (order_hbm, order_ref),
            )
        )
    ]
    for copy in small:
        copy.start()
    loads = []
    for part, owner in enumerate((me, other)):
        from_rows = pl.ds(pl.multiple_of(owner * half, half), half)
        for at, (hbm, vmem) in enumerate(((wq_hbm, wq), (wk_hbm, wk), (wv_hbm, wv))):
            loads.append(
                pltpu.make_async_copy(
                    hbm.at[from_rows, :], vmem.at[part], load_sems.at[1 + 3 * part + at]
                )
            )
    for load in loads[:3]:
        load.start()

    @pl.loop(0, device_count - 1)
    def _(step):
        pl.semaphore_signal(
            barrier, inc=1, device_id=target_of(step), device_id_type=MESH
        )

    for load in loads[3:]:
        load.start()
    load_ck = pltpu.make_async_copy(ck_hbm, ck, load_sems.at[7])
    load_cv = pltpu.make_async_copy(cv_hbm, cv, load_sems.at[8])
    load_ck.start()
    load_cv.start()

    def wo_load(at):
        side = other if at < half_chunks else me
        column = side * half + at % half_chunks * O_COLS
        return pltpu.make_async_copy(
            wo_hbm.at[:, pl.ds(pl.multiple_of(column, O_COLS), O_COLS)],
            wo.at[at],
            wo_sems.at[at],
        )

    for at in range(2 * half_chunks):
        wo_load(at).start()

    load_hid.wait()
    step_rows = 16

    @pl.loop(0, rows // step_rows, unroll=4)
    def _(block):
        at = pl.ds(pl.multiple_of(block * step_rows, step_rows), step_rows)
        total = jnp.zeros((step_rows, HEAD_SIZE), jnp.float32)
        for tile in range(half // HEAD_SIZE):
            piece = hid[at, tile * HEAD_SIZE : (tile + 1) * HEAD_SIZE].astype(jnp.float32)
            total = total + piece * piece
        squares[0, at, :] = total

    pl.semaphore_wait(barrier, device_count - 1)
    square_copy = pltpu.make_async_remote_copy(
        src_ref=squares.at[0],
        dst_ref=squares.at[1],
        send_sem=square_sems.at[0],
        recv_sem=square_sems.at[1],
        device_id=partner,
        device_id_type=MESH,
    )
    square_copy.start()

    for copy in small:
        copy.wait()
    lane64 = lax.broadcasted_iota(jnp.int32, (slots, slots), 1)
    eye64 = lax.broadcasted_iota(jnp.int32, (slots, slots), 0) == lane64
    parent_columns = []
    for p in range(requests):
        row = jnp.broadcast_to(parents_ref[p : p + 1, :].astype(jnp.float32), (slots, slots))
        parent_columns.append(
            jnp.sum(jnp.where(eye64, row, 0.0), axis=1, keepdims=True) + float(p * slots)
        )
    parent_column = jnp.concatenate(parent_columns, axis=0).astype(jnp.int32)
    row_at = lax.broadcasted_iota(jnp.int32, (rows, rows), 0)
    lane_at = lax.broadcasted_iota(jnp.int32, (rows, rows), 1)
    linked = jnp.where((lane_at == parent_column) | (row_at == lane_at), 1.0, 0.0).astype(
        jnp.bfloat16
    )
    for doubling in range(max(1, (slots - 1).bit_length())):
        linked = jnp.minimum(
            jnp.dot(linked, linked, preferred_element_type=jnp.float32), 1.0
        ).astype(jnp.bfloat16)
    fold_row = lax.broadcasted_iota(jnp.int32, (rows, slots), 0)
    fold_lane = lax.broadcasted_iota(jnp.int32, (rows, slots), 1)
    fold = jnp.where(lax.rem(fold_row, slots) == fold_lane, 1.0, 0.0).astype(jnp.bfloat16)
    anc[...] = jnp.dot(linked, fold, preferred_element_type=jnp.float32)
    row_id = lax.broadcasted_iota(jnp.int32, (rows, HEAD_SIZE), 0)
    lane_id = lax.broadcasted_iota(jnp.int32, (rows, HEAD_SIZE), 1)
    length_at = jnp.zeros((rows, HEAD_SIZE), jnp.float32)
    end_at = jnp.zeros((rows, HEAD_SIZE), jnp.int32)
    for p in range(requests):
        here = row_id // slots == p
        length_at = jnp.where(here, lengths_ref[p].astype(jnp.float32), length_at)
        end_at = jnp.where(here, counts_ref[p] + p * slots, end_at)
    live[...] = jnp.where(row_id < end_at, 1.0, 0.0)
    gain = gain_ref[...].astype(jnp.float32).reshape(1, half)

    square_copy.wait()
    for load in loads[:3]:
        load.wait()

    def norm_copy(block):
        at = pl.ds(block * norm_rows, norm_rows)
        return pltpu.make_async_remote_copy(
            src_ref=normed.at[0, at, :],
            dst_ref=normed.at[1, at, :],
            send_sem=norm_send.at[block],
            recv_sem=norm_recv.at[block],
            device_id=partner,
            device_id_type=MESH,
        )

    def normalise(block):
        for first in range(block * norm_rows, (block + 1) * norm_rows, step_rows):
            at = slice(first, first + step_rows)
            square = jnp.sum(squares[0, at, :] + squares[1, at, :], axis=1, keepdims=True)
            scale = lax.rsqrt(square / (2.0 * half) + rms_epsilon)
            normed[0, at, :] = (hid[at, :].astype(jnp.float32) * scale * gain).astype(
                jnp.bfloat16
            )
        norm_copy(block).start()

    def rotate(block, at):
        return (
            block * cosine[at, :] + pltpu.roll(block, HEAD_SIZE // 2, 1) * sine[at, :]
        ).astype(jnp.bfloat16)

    chunks = q_width // Q_COLS + 2

    def weight(part, n):
        if n < q_width // Q_COLS:
            return wq[part, :, n * Q_COLS : (n + 1) * Q_COLS]
        return (wk if n == q_width // Q_COLS else wv)[part]

    def first_pass(n, at):
        projected[n, at, :] = jnp.dot(
            normed[0, at, :], weight(0, n), preferred_element_type=jnp.float32
        )

    def second_pass(n, at):
        product = projected[n, at, :] + jnp.dot(
            normed[1, at, :], weight(1, n), preferred_element_type=jnp.float32
        )
        if n == chunks - 1:
            v_new[at, :] = product.astype(jnp.bfloat16)
            return
        for h in range(product.shape[1] // HEAD_SIZE):
            turned = rotate(product[:, h * HEAD_SIZE : (h + 1) * HEAD_SIZE], at)
            if n == chunks - 2:
                k_rot[at, h * HEAD_SIZE : (h + 1) * HEAD_SIZE] = turned
            else:
                first = n * Q_COLS + h * HEAD_SIZE
                q_rot[at, first : first + HEAD_SIZE] = turned

    half_blocks = norm_blocks // 2
    for block in range(half_blocks):
        normalise(block)
    for n in range(chunks):
        first_pass(n, sides[0])
        if n < half_blocks:
            normalise(half_blocks + n)
    depth = jnp.sum(linked.astype(jnp.float32), axis=1, keepdims=True) - 1.0
    positions = length_at + depth
    low_half = lane_id[0:mid] < HEAD_SIZE // 2
    angles = jnp.where(low_half, positions[0:mid], positions[mid:rows]) * freqs_ref[...]
    for table, value in ((cosine, jnp.cos(angles)), (sine, jnp.sin(angles))):
        turned = pltpu.roll(value, HEAD_SIZE // 2, 1)
        sign = 1.0 if table is cosine else -1.0
        table[sides[0], :] = jnp.where(low_half, sign * value, turned)
        table[sides[1], :] = jnp.where(low_half, sign * turned, value)
    for n in range(chunks):
        first_pass(n, sides[1])

    for load in loads[3:]:
        load.wait()
    for block in range(half_blocks):
        norm_copy(block).wait()
    key_chunk = q_width // Q_COLS
    order = [key_chunk, key_chunk + 1] + list(range(key_chunk))
    for n in order:
        second_pass(n, sides[0])

    factor = math.log2(math.e) / math.sqrt(HEAD_SIZE)
    contract_last = (((1,), (1,)), ((), ()))
    cache_lane = lax.broadcasted_iota(jnp.int32, (group * slots, cache_len), 1)
    slot_lane = lax.broadcasted_iota(jnp.int32, (slots, slots), 1)

    def attend(p, g):
        at = slice(p * slots, (p + 1) * slots)
        allowed = jnp.where(slot_lane < counts_ref[p], anc[at, :], 0.0)
        allowed = jnp.concatenate([allowed] * group, axis=0) > 0.5
        alive = cache_lane < lengths_ref[p]
        columns = slice(g * HEAD_SIZE, (g + 1) * HEAD_SIZE)
        pieces = []
        for h in range(group):
            head = g * group + h
            pieces.append(q_rot[at, head * HEAD_SIZE : (head + 1) * HEAD_SIZE])
        queries = jnp.concatenate(pieces, axis=0)
        cached = jnp.where(
            alive,
            lax.dot_general(
                queries, ck[p, :, columns], contract_last, preferred_element_type=jnp.float32
            ),
            masked_score,
        )
        fresh = jnp.where(
            allowed,
            lax.dot_general(
                queries, k_rot[at, columns], contract_last, preferred_element_type=jnp.float32
            ),
            masked_score,
        )
        highest = jnp.maximum(
            jnp.max(cached, axis=1, keepdims=True), jnp.max(fresh, axis=1, keepdims=True)
        )
        cached = jnp.exp2((cached - highest) * factor)
        fresh = jnp.exp2((fresh - highest) * factor)
        total = jnp.sum(cached, axis=1, keepdims=True) + jnp.sum(fresh, axis=1, keepdims=True)
        weighted = jnp.dot(
            cached.astype(jnp.bfloat16), cv[p, :, columns], preferred_element_type=jnp.float32
        ) + jnp.dot(
            fresh.astype(jnp.bfloat16), v_new[at, columns], preferred_element_type=jnp.float32
        )
        result = (weighted / total).astype(jnp.bfloat16)
        for h in range(group):
            head = g * group + h
            att[at, head * HEAD_SIZE : (head + 1) * HEAD_SIZE] = result[
                h * slots : (h + 1) * slots
            ]

    def part_copy(c, side):
        return pltpu.make_async_remote_copy(
            src_ref=part_send.at[c, sides[side], :],
            dst_ref=part_recv.at[c, sides[side], :],
            send_sem=part_send_sems.at[c, side],
            recv_sem=part_recv_sems.at[c, side],
            device_id=partner,
            device_id_type=MESH,
        )

    def send_part(c, side):
        at = sides[side]
        part_send[c, at, :] = jnp.dot(
            att[at, :], wo[c], preferred_element_type=jnp.float32
        ).astype(jnp.bfloat16)
        part_copy(c, side).start()

    def own_product(c, side):
        at = sides[side]
        own_part[c, at, :] = jnp.dot(
            att[at, :], wo[half_chunks + c], preferred_element_type=jnp.float32
        )

    def add_up(c, side):
        at = sides[side]
        features = slice(c * O_COLS, (c + 1) * O_COLS)
        summed = (
            hid[at, features].astype(jnp.float32)
            + own_part[c, at, :]
            + part_recv[c, at, :].astype(jnp.float32)
        )
        head = head_ref[features].astype(jnp.float32).reshape(1, O_COLS)
        scored = jnp.zeros((mid, HEAD_SIZE), jnp.float32)
        for part in range(O_COLS // HEAD_SIZE):
            columns = slice(part * HEAD_SIZE, (part + 1) * HEAD_SIZE)
            kept = jnp.where(live[at, :] > 0.5, summed[:, columns], 0.0).astype(jnp.bfloat16)
            out_ref[c, at, columns] = kept
            scored = scored + kept.astype(jnp.float32) * head[:, columns]
        score_acc[at, :] = scored if c == 0 else score_acc[at, :] + scored

    def interleave(longer, shorter):
        done = 0
        for at, step in enumerate(longer):
            step()
            until = (at + 1) * len(shorter) // len(longer)
            for other_step in shorter[done:until]:
                other_step()
            done = until

    attends = [
        [
            functools.partial(attend, p, g)
            for p in range(side * requests // 2, (side + 1) * requests // 2)
            for g in range(key_heads)
        ]
        for side in range(2)
    ]
    for block in range(half_blocks, norm_blocks):
        norm_copy(block).wait()
    load_ck.wait()
    load_cv.wait()
    for c in range(half_chunks):
        wo_load(c).wait()
    interleave(attends[0], [functools.partial(second_pass, n, sides[1]) for n in order])
    interleave(attends[1], [functools.partial(send_part, c, 0) for c in range(half_chunks)])
    for c in range(half_chunks):
        send_part(c, 1)
    for c in range(half_chunks):
        wo_load(half_chunks + c).wait()
    for c in range(half_chunks):
        own_product(c, 0)
    for c in range(half_chunks):
        part_copy(c, 0).wait()
    for c in range(half_chunks):
        own_product(c, 1)
        add_up(c, 0)
    for c in range(half_chunks):
        part_copy(c, 1).wait()
    for c in range(half_chunks):
        add_up(c, 1)

    per_line = HEAD_SIZE // slots
    line_row = lax.broadcasted_iota(jnp.int32, (slots, HEAD_SIZE), 0)
    line_lane = lax.broadcasted_iota(jnp.int32, (slots, HEAD_SIZE), 1)
    lines = []
    for first in range(0, requests, per_line):
        line = jnp.zeros((slots, HEAD_SIZE), jnp.float32)
        for p in range(first, first + per_line):
            column = jnp.sum(score_acc[p * slots : (p + 1) * slots, :], axis=1, keepdims=True)
            line = jnp.where(line_lane - (p - first) * slots == line_row, column, line)
        lines.append(jnp.sum(line, axis=0, keepdims=True))
    scores = jnp.concatenate(lines, axis=0)
    mine[...] = scores
    gathered[flat] = scores

    @pl.loop(0, device_count - 1)
    def _(step):
        pltpu.make_async_remote_copy(
            src_ref=mine,
            dst_ref=gathered.at[flat],
            send_sem=all_send,
            recv_sem=all_recv,
            device_id=target_of(step),
            device_id_type=MESH,
        ).start()

    per_request = accept_ref.shape[1]
    picks = requests * per_request * 2
    pick_row = lax.broadcasted_iota(jnp.int32, (picks, rows), 0)
    pick_lane = lax.broadcasted_iota(jnp.int32, (picks, rows), 1)
    wanted = jnp.zeros((picks, rows), jnp.int32)
    for p in range(requests):
        for a in range(per_request):
            wanted = jnp.where(
                pick_row // 2 == p * per_request + a, accept_ref[p, a] + p * slots, wanted
            )
    chosen = pick_lane == wanted
    odd = lax.rem(pick_row, 2) == 1
    pick_keys = jnp.where(chosen & ~odd, 1.0, 0.0).astype(jnp.bfloat16)
    pick_values = jnp.where(chosen & odd, 1.0, 0.0).astype(jnp.bfloat16)
    picked_rows = jnp.dot(
        pick_keys, k_rot[...], preferred_element_type=jnp.float32
    ) + jnp.dot(pick_values, v_new[...], preferred_element_type=jnp.float32)
    rows_ref[...] = picked_rows.reshape(rows_ref.shape).astype(jnp.bfloat16)

    everything = gathered.at[pl.ds(0, device_count - 1)]
    whole = pltpu.make_async_remote_copy(
        src_ref=everything,
        dst_ref=everything,
        send_sem=all_send,
        recv_sem=all_recv,
        device_id=partner,
        device_id_type=MESH,
    )
    whole.wait_send()
    whole.wait_recv()

    shape = (device_count, requests // per_line, HEAD_SIZE)
    source = lax.broadcasted_iota(jnp.int32, shape, 0) // narrow_count
    line_at = lax.broadcasted_iota(jnp.int32, shape, 1)
    place = lax.broadcasted_iota(jnp.int32, shape, 2) // slots
    request_at = source * requests + line_at * per_line + place
    values = gathered[...]
    for r in range(requests):
        picked = jnp.sum(jnp.where(request_at == order_ref[r], values, 0.0), axis=0)
        picked = jnp.sum(picked, axis=0, keepdims=True)
        total = picked[:, :slots]
        for part in range(1, per_line):
            total = total + picked[:, part * slots : (part + 1) * slots]
        verify_ref[r : r + 1, :] = total


def body(
    hidden_in,
    norm_gain,
    w_query,
    key_weight,
    value_weight,
    w_out,
    cached_key_rows,
    cached_value_rows,
    lengths,
    counts,
    parents,
    accept,
    order_map,
    accept_head,
):
    wide_count = lax.axis_size("wide")
    narrow_count = lax.axis_size("narrow")
    device_count = wide_count * narrow_count
    rows, half = hidden_in.shape
    requests, slots = parents.shape
    per_request = accept.shape[1]
    query_width = w_query.shape[1]
    key_width = key_weight.shape[1]
    norm_blocks = 4
    half_chunks = half // O_COLS
    q_chunks = query_width // Q_COLS
    exponents = np.arange(HEAD_SIZE) % (HEAD_SIZE // 2) * 2.0 / HEAD_SIZE
    freqs = jnp.asarray((10000.0**-exponents)[None, :].astype(np.float32))
    hbm_spec = pl.BlockSpec(memory_space=pltpu.HBM)
    vmem_spec = pl.BlockSpec(memory_space=pltpu.VMEM)
    bf16, f32 = jnp.bfloat16, jnp.float32
    hidden, picked_rows, scores = pl.pallas_call(
        functools.partial(layer_kernel, wide_count, narrow_count),
        out_shape=(
            jax.ShapeDtypeStruct((half_chunks, rows, O_COLS), bf16),
            jax.ShapeDtypeStruct((requests, per_request, 2, key_width), bf16),
            jax.ShapeDtypeStruct((requests, slots), f32),
        ),
        in_specs=[hbm_spec] * 15,
        out_specs=(vmem_spec, vmem_spec, vmem_spec),
        scratch_shapes=[
            pltpu.VMEM(norm_gain.shape, bf16),
            pltpu.VMEM(accept_head.shape, bf16),
            pltpu.VMEM(freqs.shape, f32),
            pltpu.VMEM(parents.shape, parents.dtype),
            pltpu.SMEM(lengths.shape, lengths.dtype),
            pltpu.SMEM(counts.shape, counts.dtype),
            pltpu.SMEM(accept.shape, accept.dtype),
            pltpu.SMEM(order_map.shape, order_map.dtype),
            pltpu.VMEM((rows, half), bf16),
            pltpu.VMEM((2, rows, half), bf16),
            pltpu.VMEM((2, rows, HEAD_SIZE), f32),
            pltpu.VMEM((2, half, query_width), bf16),
            pltpu.VMEM((2, half, key_width), bf16),
            pltpu.VMEM((2, half, key_width), bf16),
            pltpu.VMEM((2 * half_chunks, query_width, O_COLS), bf16),
            pltpu.VMEM(cached_key_rows.shape, bf16),
            pltpu.VMEM(cached_value_rows.shape, bf16),
            pltpu.VMEM((q_chunks + 2, rows, Q_COLS), f32),
            pltpu.VMEM((half_chunks, rows, O_COLS), f32),
            pltpu.VMEM((rows, slots), f32),
            pltpu.VMEM((rows, HEAD_SIZE), f32),
            pltpu.VMEM((rows, HEAD_SIZE), f32),
            pltpu.VMEM((rows, HEAD_SIZE), f32),
            pltpu.VMEM((rows, query_width), bf16),
            pltpu.VMEM((rows, key_width), bf16),
            pltpu.VMEM((rows, key_width), bf16),
            pltpu.VMEM((rows, query_width), bf16),
            pltpu.VMEM((half_chunks, rows, O_COLS), bf16),
            pltpu.VMEM((half_chunks, rows, O_COLS), bf16),
            pltpu.VMEM((rows, HEAD_SIZE), f32),
            pltpu.VMEM((requests * slots // HEAD_SIZE, HEAD_SIZE), f32),
            pltpu.VMEM((device_count, requests * slots // HEAD_SIZE, HEAD_SIZE), f32),
            pltpu.SemaphoreType.DMA((8,)),
            pltpu.SemaphoreType.DMA((9,)),
            pltpu.SemaphoreType.DMA((2 * half_chunks,)),
            pltpu.SemaphoreType.DMA((2,)),
            pltpu.SemaphoreType.DMA((norm_blocks,)),
            pltpu.SemaphoreType.DMA((norm_blocks,)),
            pltpu.SemaphoreType.DMA((half_chunks, 2)),
            pltpu.SemaphoreType.DMA((half_chunks, 2)),
            pltpu.SemaphoreType.DMA,
            pltpu.SemaphoreType.DMA,
        ],
        compiler_params=pltpu.CompilerParams(
            collective_id=0, has_side_effects=True, vmem_limit_bytes=48 * 2**20
        ),
    )(
        *(
            pltpu.with_memory_space_constraint(operand, pltpu.HBM)
            for operand in (
                hidden_in,
                norm_gain,
                accept_head,
                freqs,
                w_query,
                key_weight,
                value_weight,
                w_out,
                cached_key_rows,
                cached_value_rows,
                parents,
                lengths,
                counts,
                accept,
                order_map,
            )
        )
    )
    return pl.pallas_call(
        finish_kernel,
        out_shape=(
            jax.ShapeDtypeStruct((rows, half), bf16),
            jax.ShapeDtypeStruct((requests, per_request, 2, key_width), bf16),
            jax.ShapeDtypeStruct((requests, slots), f32),
        ),
        in_specs=[vmem_spec, vmem_spec, vmem_spec],
        out_specs=(hbm_spec, hbm_spec, hbm_spec),
        scratch_shapes=[pltpu.SemaphoreType.DMA((half_chunks + 2,))],
        compiler_params=pltpu.CompilerParams(vmem_limit_bytes=8 * 2**20),
    )(hidden, picked_rows, scores)


def solution(mesh):
    placed = (
        P("wide", "narrow"),
        P("narrow"),
        P(None, "narrow"),
        P(None, "narrow"),
        P(None, "narrow"),
        P("narrow", None),
        P("wide", None, "narrow"),
        P("wide", None, "narrow"),
        P("wide"),
        P("wide"),
        P("wide", None),
        P("wide", None),
        P("wide"),
        P("narrow"),
    )
    return jax.shard_map(
        body,
        mesh=mesh,
        in_specs=placed,
        out_specs=(P("wide", "narrow"), P("wide", None, None, "narrow"), P("wide", None)),
        check_vma=False,
    )
```

```python
import functools
import math

import jax
import jax.numpy as jnp
import numpy as np
from jax import lax
from jax.experimental import pallas as pl
from jax.experimental.pallas import tpu as pltpu
from jax.sharding import PartitionSpec as P

HEAD_SIZE = 128
MESH = pl.DeviceIdType.MESH
Q_COLS = 256
O_COLS = 512

masked_score = -1e30
keep_score = 3e38
rms_epsilon = 1e-05


def finish_kernel(
    hidden_ref, rows_ref, scores_ref, out_ref, new_rows_ref, verify_ref, out_sems
):
    pieces = hidden_ref.shape[0]
    stores = [
        pltpu.make_async_copy(
            hidden_ref.at[n], out_ref.at[:, pl.ds(n * O_COLS, O_COLS)], out_sems.at[n]
        )
        for n in range(pieces)
    ]
    stores.append(pltpu.make_async_copy(rows_ref, new_rows_ref, out_sems.at[pieces]))
    stores.append(pltpu.make_async_copy(scores_ref, verify_ref, out_sems.at[pieces + 1]))
    for store in stores:
        store.start()
    for store in stores:
        store.wait()


def layer_kernel(
    wide_count,
    narrow_count,
    hidden_hbm,
    gain_hbm,
    head_hbm,
    freqs_hbm,
    wq_hbm,
    wk_hbm,
    wv_hbm,
    wo_hbm,
    ck_hbm,
    cv_hbm,
    parents_hbm,
    lengths_hbm,
    counts_hbm,
    accept_hbm,
    order_hbm,
    out_ref,
    rows_ref,
    verify_ref,
    gain_ref,
    head_ref,
    freqs_ref,
    parents_ref,
    lengths_ref,
    counts_ref,
    accept_ref,
    order_ref,
    hid,
    normed,
    squares,
    wq,
    wk,
    wv,
    wo,
    ck,
    cv,
    projected,
    own_part,
    caps,
    cache_scores,
    slot_scores,
    cache_probs,
    slot_probs,
    totals,
    cosine,
    sine,
    live,
    q_rot,
    k_rot,
    v_new,
    att,
    part_send,
    part_recv,
    score_acc,
    mine,
    gathered,
    small_sems,
    load_sems,
    wo_sems,
    square_sems,
    norm_send,
    norm_recv,
    part_send_sems,
    part_recv_sems,
    all_send,
    all_recv,
):
    me_wide = lax.axis_index("wide")
    me = lax.axis_index("narrow")
    other = 1 - me
    device_count = wide_count * narrow_count
    flat = me_wide * narrow_count + me
    rows, half = hid.shape
    requests, slots = parents_ref.shape
    q_width = wq_hbm.shape[1]
    half_chunks = half // O_COLS
    key_heads = wk_hbm.shape[1] // HEAD_SIZE
    group = q_width // HEAD_SIZE // key_heads
    cache_len = ck.shape[1]
    partner = (me_wide, other)
    norm_blocks = norm_send.shape[0]
    norm_rows = rows // norm_blocks
    mid = rows // 2
    sides = (slice(0, mid), slice(mid, rows))

    def target_of(step):
        target = step + jnp.where(step >= flat, 1, 0)
        return (target // narrow_count, lax.rem(target, narrow_count))

    barrier = pltpu.get_barrier_semaphore()
    load_hid = [
        pltpu.make_async_copy(
            hidden_hbm.at[pl.ds(side * mid, mid), :],
            hid.at[pl.ds(side * mid, mid), :],
            load_sems.at[9 * side],
        )
        for side in range(2)
    ]
    for load in load_hid:
        load.start()
    small = [
        pltpu.make_async_copy(hbm, there, small_sems.at[at])
        for at, (hbm, there) in enumerate(
            (
                (parents_hbm, parents_ref),
                (gain_hbm, gain_ref),
                (freqs_hbm, freqs_ref),
                (head_hbm, head_ref),
                (lengths_hbm, lengths_ref),
                (counts_hbm, counts_ref),
                (accept_hbm, accept_ref),
                (order_hbm, order_ref),
            )
        )
    ]
    for copy in small:
        copy.start()
    loads = []
    for part, owner in enumerate((me, other)):
        from_rows = pl.ds(pl.multiple_of(owner * half, half), half)
        for at, (hbm, vmem) in enumerate(((wq_hbm, wq), (wk_hbm, wk), (wv_hbm, wv))):
            loads.append(
                pltpu.make_async_copy(
                    hbm.at[from_rows, :], vmem.at[part], load_sems.at[1 + 3 * part + at]
                )
            )
    for load in loads[:3]:
        load.start()

    @pl.loop(0, device_count - 1, unroll=8)
    def _(step):
        pl.semaphore_signal(
            barrier, inc=1, device_id=target_of(step), device_id_type=MESH
        )

    for load in loads[3:]:
        load.start()
    load_ck = pltpu.make_async_copy(ck_hbm, ck, load_sems.at[7])
    load_cv = pltpu.make_async_copy(cv_hbm, cv, load_sems.at[8])
    load_ck.start()
    load_cv.start()

    def wo_load(at):
        side = other if at < half_chunks else me
        column = side * half + at % half_chunks * O_COLS
        return pltpu.make_async_copy(
            wo_hbm.at[:, pl.ds(pl.multiple_of(column, O_COLS), O_COLS)],
            wo.at[at],
            wo_sems.at[at],
        )

    step_rows = 16

    def square_up(side):
        load_hid[side].wait()

        @pl.loop(side * mid // step_rows, (side + 1) * mid // step_rows, unroll=4)
        def _(block):
            at = pl.ds(pl.multiple_of(block * step_rows, step_rows), step_rows)
            total = jnp.zeros((step_rows, HEAD_SIZE), jnp.float32)
            for tile in range(half // HEAD_SIZE):
                piece = hid[at, tile * HEAD_SIZE : (tile + 1) * HEAD_SIZE].astype(jnp.float32)
                total = total + piece * piece
            squares[0, at, :] = total

    square_copies = [
        pltpu.make_async_remote_copy(
            src_ref=squares.at[0, pl.ds(side * mid, mid), :],
            dst_ref=squares.at[1, pl.ds(side * mid, mid), :],
            send_sem=square_sems.at[side, 0],
            recv_sem=square_sems.at[side, 1],
            device_id=partner,
            device_id_type=MESH,
        )
        for side in range(2)
    ]
    square_up(0)
    pl.semaphore_wait(barrier, device_count - 1)
    square_copies[0].start()
    square_up(1)
    square_copies[1].start()

    for copy in small:
        copy.wait()
    lane64 = lax.broadcasted_iota(jnp.int32, (slots, slots), 1)
    eye64 = lax.broadcasted_iota(jnp.int32, (slots, slots), 0) == lane64
    parent_columns = []
    for p in range(requests):
        row = jnp.broadcast_to(parents_ref[p : p + 1, :].astype(jnp.float32), (slots, slots))
        parent_columns.append(
            jnp.sum(jnp.where(eye64, row, 0.0), axis=1, keepdims=True) + float(p * slots)
        )
    parent_column = jnp.concatenate(parent_columns, axis=0).astype(jnp.int32)
    row_at = lax.broadcasted_iota(jnp.int32, (rows, rows), 0)
    lane_at = lax.broadcasted_iota(jnp.int32, (rows, rows), 1)
    linked = jnp.where((lane_at == parent_column) | (row_at == lane_at), 1.0, 0.0).astype(
        jnp.bfloat16
    )
    for doubling in range(max(1, (slots - 1).bit_length())):
        linked = jnp.minimum(
            jnp.dot(linked, linked, preferred_element_type=jnp.float32), 1.0
        ).astype(jnp.bfloat16)
    row_id = lax.broadcasted_iota(jnp.int32, (rows, HEAD_SIZE), 0)
    lane_id = lax.broadcasted_iota(jnp.int32, (rows, HEAD_SIZE), 1)
    length_at = jnp.zeros((rows, HEAD_SIZE), jnp.float32)
    end_at = jnp.zeros((rows, HEAD_SIZE), jnp.int32)
    for p in range(requests):
        here = row_id // slots == p
        length_at = jnp.where(here, lengths_ref[p].astype(jnp.float32), length_at)
        end_at = jnp.where(here, counts_ref[p] + p * slots, end_at)
    live[...] = jnp.where(row_id < end_at, 1.0, 0.0)
    for side in sides:
        slot_at = lax.broadcasted_iota(jnp.int32, (mid, mid), 1) + side.start
        within = jnp.where(slot_at < end_at[side], linked[side, side].astype(jnp.float32), 0.0)
        caps[side, :] = jnp.where(within > 0.5, keep_score, masked_score)
    gain = gain_ref[...].astype(jnp.float32).reshape(1, half)

    for at in range(2 * half_chunks):
        wo_load(at).start()

    square_copies[0].wait()
    for load in loads[:3]:
        load.wait()

    def norm_copy(block):
        at = pl.ds(block * norm_rows, norm_rows)
        return pltpu.make_async_remote_copy(
            src_ref=normed.at[0, at, :],
            dst_ref=normed.at[1, at, :],
            send_sem=norm_send.at[block],
            recv_sem=norm_recv.at[block],
            device_id=partner,
            device_id_type=MESH,
        )

    def normalise(block):
        for first in range(block * norm_rows, (block + 1) * norm_rows, step_rows):
            at = slice(first, first + step_rows)
            square = jnp.sum(squares[0, at, :] + squares[1, at, :], axis=1, keepdims=True)
            scale = lax.rsqrt(square / (2.0 * half) + rms_epsilon)
            normed[0, at, :] = (hid[at, :].astype(jnp.float32) * scale * gain).astype(
                jnp.bfloat16
            )
        norm_copy(block).start()

    def rotate(block, at):
        return (
            block * cosine[at, :] + pltpu.roll(block, HEAD_SIZE // 2, 1) * sine[at, :]
        ).astype(jnp.bfloat16)

    chunks = q_width // Q_COLS + 2

    def weight(part, n):
        if n < q_width // Q_COLS:
            return wq[part, :, n * Q_COLS : (n + 1) * Q_COLS]
        return (wk if n == q_width // Q_COLS else wv)[part]

    def first_pass(n, at):
        projected[n, at, :] = jnp.dot(
            normed[0, at, :], weight(0, n), preferred_element_type=jnp.float32
        )

    def second_pass(n, at):
        product = projected[n, at, :] + jnp.dot(
            normed[1, at, :], weight(1, n), preferred_element_type=jnp.float32
        )
        if n == chunks - 1:
            v_new[at, :] = product.astype(jnp.bfloat16)
            return
        for h in range(product.shape[1] // HEAD_SIZE):
            turned = rotate(product[:, h * HEAD_SIZE : (h + 1) * HEAD_SIZE], at)
            if n == chunks - 2:
                k_rot[at, h * HEAD_SIZE : (h + 1) * HEAD_SIZE] = turned
            else:
                first = n * Q_COLS + h * HEAD_SIZE
                q_rot[at, first : first + HEAD_SIZE] = turned

    half_blocks = norm_blocks // 2
    for block in range(half_blocks):
        normalise(block)
    square_copies[1].wait()
    for n in range(chunks):
        first_pass(n, sides[0])
        if n < half_blocks:
            normalise(half_blocks + n)
    depth = jnp.sum(linked.astype(jnp.float32), axis=1, keepdims=True) - 1.0
    positions = length_at + depth
    low_half = lane_id[0:mid] < HEAD_SIZE // 2
    angles = jnp.where(low_half, positions[0:mid], positions[mid:rows]) * freqs_ref[...]
    for table, value in ((cosine, jnp.cos(angles)), (sine, jnp.sin(angles))):
        turned = pltpu.roll(value, HEAD_SIZE // 2, 1)
        sign = 1.0 if table is cosine else -1.0
        table[sides[0], :] = jnp.where(low_half, sign * value, turned)
        table[sides[1], :] = jnp.where(low_half, sign * turned, value)
    for n in range(chunks):
        first_pass(n, sides[1])

    for load in loads[3:]:
        load.wait()
    for block in range(half_blocks):
        norm_copy(block).wait()
    key_chunk = q_width // Q_COLS
    order = [key_chunk, key_chunk + 1] + list(range(key_chunk))
    for n in order:
        second_pass(n, sides[0])

    factor = math.log2(math.e) / math.sqrt(HEAD_SIZE)
    contract_last = (((1,), (1,)), ((), ()))
    cache_lane = lax.broadcasted_iota(jnp.int32, (1, cache_len), 1)
    steps = [(p, g) for p in range(requests) for g in range(key_heads)]

    def places(i):
        p, g = steps[i]
        pair = slice(p * slots // mid * mid, p * slots // mid * mid + mid)
        return p, g, slice(p * slots, (p + 1) * slots), pair, slice(g * HEAD_SIZE, (g + 1) * HEAD_SIZE)

    def score(i):
        p, g, at, pair, columns = places(i)
        pieces = []
        for h in range(group):
            head = g * group + h
            pieces.append(q_rot[at, head * HEAD_SIZE : (head + 1) * HEAD_SIZE])
        queries = jnp.concatenate(pieces, axis=0)
        cache_scores[i] = lax.dot_general(
            queries, ck[p, :, columns], contract_last, preferred_element_type=jnp.float32
        )
        slot_scores[i] = lax.dot_general(
            queries, k_rot[pair, columns], contract_last, preferred_element_type=jnp.float32
        )

    def soften(i):
        p, g, at, pair, columns = places(i)
        cache_cap = jnp.where(cache_lane < lengths_ref[p], keep_score, masked_score)
        slot_cap = jnp.concatenate([caps[at, :]] * group, axis=0)
        tiles = [
            jnp.minimum(cache_scores[i, :, t : t + HEAD_SIZE], cache_cap[:, t : t + HEAD_SIZE])
            for t in range(0, cache_len, HEAD_SIZE)
        ]
        tiles.append(jnp.minimum(slot_scores[i], slot_cap))
        highest = functools.reduce(jnp.maximum, tiles)
        highest = jnp.max(highest, axis=1, keepdims=True)
        tiles = [jnp.exp2((tile - highest) * factor) for tile in tiles]
        total = jnp.sum(functools.reduce(jnp.add, tiles), axis=1, keepdims=True)
        totals[i] = jnp.broadcast_to(total, totals.shape[1:])
        for t, tile in enumerate(tiles[:-1]):
            cache_probs[i, :, t * HEAD_SIZE : (t + 1) * HEAD_SIZE] = tile.astype(jnp.bfloat16)
        slot_probs[i] = tiles[-1].astype(jnp.bfloat16)

    def collect(i):
        p, g, at, pair, columns = places(i)
        weighted = jnp.dot(
            cache_probs[i], cv[p, :, columns], preferred_element_type=jnp.float32
        ) + jnp.dot(slot_probs[i], v_new[pair, columns], preferred_element_type=jnp.float32)
        result = (weighted / totals[i]).astype(jnp.bfloat16)
        for h in range(group):
            head = g * group + h
            att[at, head * HEAD_SIZE : (head + 1) * HEAD_SIZE] = result[
                h * slots : (h + 1) * slots
            ]

    def part_copy(c, side):
        return pltpu.make_async_remote_copy(
            src_ref=part_send.at[c, sides[side], :],
            dst_ref=part_recv.at[c, sides[side], :],
            send_sem=part_send_sems.at[c, side],
            recv_sem=part_recv_sems.at[c, side],
            device_id=partner,
            device_id_type=MESH,
        )

    def send_part(c, side):
        at = sides[side]
        part_send[c, at, :] = jnp.dot(
            att[at, :], wo[c], preferred_element_type=jnp.float32
        ).astype(jnp.bfloat16)

    def own_product(c, side):
        at = sides[side]
        own_part[c, at, :] = jnp.dot(
            att[at, :], wo[half_chunks + c], preferred_element_type=jnp.float32
        )

    def add_up(c, side):
        at = sides[side]
        features = slice(c * O_COLS, (c + 1) * O_COLS)
        summed = (
            hid[at, features].astype(jnp.float32)
            + own_part[c, at, :]
            + part_recv[c, at, :].astype(jnp.float32)
        )
        head = head_ref[features].astype(jnp.float32).reshape(1, O_COLS)
        scored = jnp.zeros((mid, HEAD_SIZE), jnp.float32)
        for part in range(O_COLS // HEAD_SIZE):
            columns = slice(part * HEAD_SIZE, (part + 1) * HEAD_SIZE)
            kept = jnp.where(live[at, :] > 0.5, summed[:, columns], 0.0).astype(jnp.bfloat16)
            out_ref[c, at, columns] = kept
            scored = scored + kept.astype(jnp.float32) * head[:, columns]
        score_acc[at, :] = scored if c == 0 else score_acc[at, :] + scored

    for block in range(half_blocks, norm_blocks):
        norm_copy(block).wait()
    load_ck.wait()
    load_cv.wait()
    score(0)
    score(1)
    middle = len(steps) // 2
    pending = list(order)
    for i in range(len(steps)):
        if i == middle:
            for c in range(half_chunks):
                wo_load(c).wait()
        soften(i)
        for n in pending[: -(-len(order) // max(middle - 1, 1))]:
            pending.remove(n)
            second_pass(n, sides[1])
        if i + 2 < len(steps):
            score(i + 2)
        if i > 0:
            collect(i - 1)
        if i == middle:
            for c in range(half_chunks):
                send_part(c, 0)
            for c in range(half_chunks):
                part_copy(c, 0).start()
    collect(len(steps) - 1)
    for first in range(0, half_chunks, 2):
        for c in range(first, first + 2):
            send_part(c, 1)
        for c in range(first, first + 2):
            part_copy(c, 1).start()
    for c in range(half_chunks):
        wo_load(half_chunks + c).wait()
    for c in range(half_chunks):
        own_product(c, 0)
    for c in range(half_chunks):
        part_copy(c, 0).wait()
    for c in range(half_chunks):
        own_product(c, 1)
        add_up(c, 0)
    for c in range(half_chunks):
        part_copy(c, 1).wait()
    for c in range(half_chunks):
        add_up(c, 1)

    per_line = HEAD_SIZE // slots
    line_row = lax.broadcasted_iota(jnp.int32, (slots, HEAD_SIZE), 0)
    line_lane = lax.broadcasted_iota(jnp.int32, (slots, HEAD_SIZE), 1)
    lines = []
    for first in range(0, requests, per_line):
        line = jnp.zeros((slots, HEAD_SIZE), jnp.float32)
        for p in range(first, first + per_line):
            column = jnp.sum(score_acc[p * slots : (p + 1) * slots, :], axis=1, keepdims=True)
            line = jnp.where(line_lane - (p - first) * slots == line_row, column, line)
        lines.append(jnp.sum(line, axis=0, keepdims=True))
    scores = jnp.concatenate(lines, axis=0)
    mine[...] = scores
    gathered[flat] = scores

    @pl.loop(0, device_count - 1, unroll=8)
    def _(step):
        pltpu.make_async_remote_copy(
            src_ref=mine,
            dst_ref=gathered.at[flat],
            send_sem=all_send,
            recv_sem=all_recv,
            device_id=target_of(step),
            device_id_type=MESH,
        ).start()

    per_request = accept_ref.shape[1]
    picks = requests * per_request * 2
    pick_row = lax.broadcasted_iota(jnp.int32, (picks, rows), 0)
    pick_lane = lax.broadcasted_iota(jnp.int32, (picks, rows), 1)
    wanted = jnp.zeros((picks, rows), jnp.int32)
    for p in range(requests):
        for a in range(per_request):
            wanted = jnp.where(
                pick_row // 2 == p * per_request + a, accept_ref[p, a] + p * slots, wanted
            )
    chosen = pick_lane == wanted
    odd = lax.rem(pick_row, 2) == 1
    pick_keys = jnp.where(chosen & ~odd, 1.0, 0.0).astype(jnp.bfloat16)
    pick_values = jnp.where(chosen & odd, 1.0, 0.0).astype(jnp.bfloat16)
    picked_rows = jnp.dot(
        pick_keys, k_rot[...], preferred_element_type=jnp.float32
    ) + jnp.dot(pick_values, v_new[...], preferred_element_type=jnp.float32)
    rows_ref[...] = picked_rows.reshape(rows_ref.shape).astype(jnp.bfloat16)

    everything = gathered.at[pl.ds(0, device_count - 1)]
    whole = pltpu.make_async_remote_copy(
        src_ref=everything,
        dst_ref=everything,
        send_sem=all_send,
        recv_sem=all_recv,
        device_id=partner,
        device_id_type=MESH,
    )
    whole.wait_send()
    whole.wait_recv()

    shape = (device_count, requests // per_line, HEAD_SIZE)
    source = lax.broadcasted_iota(jnp.int32, shape, 0) // narrow_count
    line_at = lax.broadcasted_iota(jnp.int32, shape, 1)
    place = lax.broadcasted_iota(jnp.int32, shape, 2) // slots
    request_at = source * requests + line_at * per_line + place
    values = gathered[...]
    for r in range(requests):
        picked = jnp.sum(jnp.where(request_at == order_ref[r], values, 0.0), axis=0)
        picked = jnp.sum(picked, axis=0, keepdims=True)
        total = picked[:, :slots]
        for part in range(1, per_line):
            total = total + picked[:, part * slots : (part + 1) * slots]
        verify_ref[r : r + 1, :] = total


def body(
    hidden_in,
    norm_gain,
    w_query,
    key_weight,
    value_weight,
    w_out,
    cached_key_rows,
    cached_value_rows,
    lengths,
    counts,
    parents,
    accept,
    order_map,
    accept_head,
):
    wide_count = lax.axis_size("wide")
    narrow_count = lax.axis_size("narrow")
    device_count = wide_count * narrow_count
    rows, half = hidden_in.shape
    requests, slots = parents.shape
    per_request = accept.shape[1]
    query_width = w_query.shape[1]
    key_width = key_weight.shape[1]
    norm_blocks = 4
    key_heads = key_width // HEAD_SIZE
    steps = requests * key_heads
    grouped = query_width // key_width * slots
    cache_len = cached_key_rows.shape[1]
    half_chunks = half // O_COLS
    q_chunks = query_width // Q_COLS
    exponents = np.arange(HEAD_SIZE) % (HEAD_SIZE // 2) * 2.0 / HEAD_SIZE
    freqs = jnp.asarray((10000.0**-exponents)[None, :].astype(np.float32))
    hbm_spec = pl.BlockSpec(memory_space=pltpu.HBM)
    vmem_spec = pl.BlockSpec(memory_space=pltpu.VMEM)
    bf16, f32 = jnp.bfloat16, jnp.float32
    hidden, picked_rows, scores = pl.pallas_call(
        functools.partial(layer_kernel, wide_count, narrow_count),
        out_shape=(
            jax.ShapeDtypeStruct((half_chunks, rows, O_COLS), bf16),
            jax.ShapeDtypeStruct((requests, per_request, 2, key_width), bf16),
            jax.ShapeDtypeStruct((requests, slots), f32),
        ),
        in_specs=[hbm_spec] * 15,
        out_specs=(vmem_spec, vmem_spec, vmem_spec),
        scratch_shapes=[
            pltpu.VMEM(norm_gain.shape, bf16),
            pltpu.VMEM(accept_head.shape, bf16),
            pltpu.VMEM(freqs.shape, f32),
            pltpu.VMEM(parents.shape, parents.dtype),
            pltpu.SMEM(lengths.shape, lengths.dtype),
            pltpu.SMEM(counts.shape, counts.dtype),
            pltpu.SMEM(accept.shape, accept.dtype),
            pltpu.SMEM(order_map.shape, order_map.dtype),
            pltpu.VMEM((rows, half), bf16),
            pltpu.VMEM((2, rows, half), bf16),
            pltpu.VMEM((2, rows, HEAD_SIZE), f32),
            pltpu.VMEM((2, half, query_width), bf16),
            pltpu.VMEM((2, half, key_width), bf16),
            pltpu.VMEM((2, half, key_width), bf16),
            pltpu.VMEM((2 * half_chunks, query_width, O_COLS), bf16),
            pltpu.VMEM(cached_key_rows.shape, bf16),
            pltpu.VMEM(cached_value_rows.shape, bf16),
            pltpu.VMEM((q_chunks + 2, rows, Q_COLS), f32),
            pltpu.VMEM((half_chunks, rows, O_COLS), f32),
            pltpu.VMEM((rows, rows // 2), f32),
            pltpu.VMEM((steps, grouped, cache_len), f32),
            pltpu.VMEM((steps, grouped, rows // 2), f32),
            pltpu.VMEM((steps, grouped, cache_len), bf16),
            pltpu.VMEM((steps, grouped, rows // 2), bf16),
            pltpu.VMEM((steps, grouped, HEAD_SIZE), f32),
            pltpu.VMEM((rows, HEAD_SIZE), f32),
            pltpu.VMEM((rows, HEAD_SIZE), f32),
            pltpu.VMEM((rows, HEAD_SIZE), f32),
            pltpu.VMEM((rows, query_width), bf16),
            pltpu.VMEM((rows, key_width), bf16),
            pltpu.VMEM((rows, key_width), bf16),
            pltpu.VMEM((rows, query_width), bf16),
            pltpu.VMEM((half_chunks, rows, O_COLS), bf16),
            pltpu.VMEM((half_chunks, rows, O_COLS), bf16),
            pltpu.VMEM((rows, HEAD_SIZE), f32),
            pltpu.VMEM((requests * slots // HEAD_SIZE, HEAD_SIZE), f32),
            pltpu.VMEM((device_count, requests * slots // HEAD_SIZE, HEAD_SIZE), f32),
            pltpu.SemaphoreType.DMA((8,)),
            pltpu.SemaphoreType.DMA((10,)),
            pltpu.SemaphoreType.DMA((2 * half_chunks,)),
            pltpu.SemaphoreType.DMA((2, 2)),
            pltpu.SemaphoreType.DMA((norm_blocks,)),
            pltpu.SemaphoreType.DMA((norm_blocks,)),
            pltpu.SemaphoreType.DMA((half_chunks, 2)),
            pltpu.SemaphoreType.DMA((half_chunks, 2)),
            pltpu.SemaphoreType.DMA,
            pltpu.SemaphoreType.DMA,
        ],
        compiler_params=pltpu.CompilerParams(
            collective_id=0, has_side_effects=True, vmem_limit_bytes=50 * 2**20
        ),
    )(
        *(
            pltpu.with_memory_space_constraint(operand, pltpu.HBM)
            for operand in (
                hidden_in,
                norm_gain,
                accept_head,
                freqs,
                w_query,
                key_weight,
                value_weight,
                w_out,
                cached_key_rows,
                cached_value_rows,
                parents,
                lengths,
                counts,
                accept,
                order_map,
            )
        )
    )
    return pl.pallas_call(
        finish_kernel,
        out_shape=(
            jax.ShapeDtypeStruct((rows, half), bf16),
            jax.ShapeDtypeStruct((requests, per_request, 2, key_width), bf16),
            jax.ShapeDtypeStruct((requests, slots), f32),
        ),
        in_specs=[vmem_spec, vmem_spec, vmem_spec],
        out_specs=(hbm_spec, hbm_spec, hbm_spec),
        scratch_shapes=[pltpu.SemaphoreType.DMA((half_chunks + 2,))],
        compiler_params=pltpu.CompilerParams(vmem_limit_bytes=8 * 2**20),
    )(hidden, picked_rows, scores)


def solution(mesh):
    placed = (
        P("wide", "narrow"),
        P("narrow"),
        P(None, "narrow"),
        P(None, "narrow"),
        P(None, "narrow"),
        P("narrow", None),
        P("wide", None, "narrow"),
        P("wide", None, "narrow"),
        P("wide"),
        P("wide"),
        P("wide", None),
        P("wide", None),
        P("wide"),
        P("narrow"),
    )
    return jax.shard_map(
        body,
        mesh=mesh,
        in_specs=placed,
        out_specs=(P("wide", "narrow"), P("wide", None, None, "narrow"), P("wide", None)),
        check_vma=False,
    )
```

```python
import functools
import math

import jax
import jax.numpy as jnp
import numpy as np
from jax import lax
from jax.experimental import pallas as pl
from jax.experimental.pallas import tpu as pltpu
from jax.sharding import PartitionSpec as P

HEAD_SIZE = 128
MESH = pl.DeviceIdType.MESH
Q_COLS = 256
O_COLS = 512

masked_score = -1e30
keep_score = 3e38
rms_epsilon = 1e-05


def finish_kernel(
    hidden_ref, rows_ref, scores_ref, out_ref, new_rows_ref, verify_ref, out_sems
):
    pieces = hidden_ref.shape[0]
    stores = [
        pltpu.make_async_copy(
            hidden_ref.at[n], out_ref.at[:, pl.ds(n * O_COLS, O_COLS)], out_sems.at[n]
        )
        for n in range(pieces)
    ]
    stores.append(pltpu.make_async_copy(rows_ref, new_rows_ref, out_sems.at[pieces]))
    stores.append(pltpu.make_async_copy(scores_ref, verify_ref, out_sems.at[pieces + 1]))
    for store in stores:
        store.start()
    for store in stores:
        store.wait()


def layer_kernel(
    wide_count,
    narrow_count,
    hidden_hbm,
    gain_hbm,
    head_hbm,
    freqs_hbm,
    wq_hbm,
    wk_hbm,
    wv_hbm,
    wo_hbm,
    ck_hbm,
    cv_hbm,
    parents_hbm,
    lengths_hbm,
    counts_hbm,
    accept_hbm,
    order_hbm,
    out_ref,
    rows_ref,
    verify_ref,
    gain_ref,
    head_ref,
    freqs_ref,
    parents_ref,
    lengths_ref,
    counts_ref,
    accept_ref,
    order_ref,
    hid,
    normed,
    squares,
    wq,
    wk,
    wv,
    wo,
    ck,
    cv,
    projected,
    own_part,
    reach,
    caps,
    cache_scores,
    slot_scores,
    cache_probs,
    slot_probs,
    totals,
    cosine,
    sine,
    live,
    q_rot,
    k_rot,
    v_new,
    att,
    part_send,
    part_recv,
    score_acc,
    mine,
    gathered,
    small_sems,
    load_sems,
    wo_sems,
    square_sems,
    norm_send,
    norm_recv,
    part_send_sems,
    part_recv_sems,
    all_send,
    all_recv,
):
    me_wide = lax.axis_index("wide")
    me = lax.axis_index("narrow")
    other = 1 - me
    device_count = wide_count * narrow_count
    flat = me_wide * narrow_count + me
    rows, half = hid.shape
    requests, slots = parents_ref.shape
    q_width = wq_hbm.shape[1]
    half_chunks = half // O_COLS
    key_heads = wk_hbm.shape[1] // HEAD_SIZE
    group = q_width // HEAD_SIZE // key_heads
    cache_len = ck.shape[1]
    partner = (me_wide, other)
    norm_blocks = norm_send.shape[0]
    norm_rows = rows // norm_blocks
    mid = rows // 2
    sides = (slice(0, mid), slice(mid, rows))

    def target_of(step):
        target = step + jnp.where(step >= flat, 1, 0)
        return (target // narrow_count, lax.rem(target, narrow_count))

    barrier = pltpu.get_barrier_semaphore()
    load_hid = [
        pltpu.make_async_copy(
            hidden_hbm.at[pl.ds(side * mid, mid), :],
            hid.at[pl.ds(side * mid, mid), :],
            load_sems.at[9 * side],
        )
        for side in range(2)
    ]
    for load in load_hid:
        load.start()
    small = [
        pltpu.make_async_copy(hbm, there, small_sems.at[at])
        for at, (hbm, there) in enumerate(
            (
                (parents_hbm, parents_ref),
                (gain_hbm, gain_ref),
                (freqs_hbm, freqs_ref),
                (head_hbm, head_ref),
                (lengths_hbm, lengths_ref),
                (counts_hbm, counts_ref),
                (accept_hbm, accept_ref),
                (order_hbm, order_ref),
            )
        )
    ]
    for copy in small:
        copy.start()
    loads = []
    for part, owner in enumerate((me, other)):
        from_rows = pl.ds(pl.multiple_of(owner * half, half), half)
        for at, (hbm, vmem) in enumerate(((wq_hbm, wq), (wk_hbm, wk), (wv_hbm, wv))):
            loads.append(
                pltpu.make_async_copy(
                    hbm.at[from_rows, :], vmem.at[part], load_sems.at[1 + 3 * part + at]
                )
            )
    for load in loads[:3]:
        load.start()

    @pl.loop(0, device_count - 1, unroll=8)
    def _(step):
        pl.semaphore_signal(
            barrier, inc=1, device_id=target_of(step), device_id_type=MESH
        )

    for load in loads[3:]:
        load.start()
    load_ck = pltpu.make_async_copy(ck_hbm, ck, load_sems.at[7])
    load_cv = pltpu.make_async_copy(cv_hbm, cv, load_sems.at[8])
    load_ck.start()
    load_cv.start()

    def wo_load(at):
        side = other if at < half_chunks else me
        column = side * half + at % half_chunks * O_COLS
        return pltpu.make_async_copy(
            wo_hbm.at[:, pl.ds(pl.multiple_of(column, O_COLS), O_COLS)],
            wo.at[at],
            wo_sems.at[at],
        )

    step_rows = 16

    def square_up(side):
        load_hid[side].wait()

        @pl.loop(side * mid // step_rows, (side + 1) * mid // step_rows, unroll=4)
        def _(block):
            at = pl.ds(pl.multiple_of(block * step_rows, step_rows), step_rows)
            total = jnp.zeros((step_rows, HEAD_SIZE), jnp.float32)
            for tile in range(half // HEAD_SIZE):
                piece = hid[at, tile * HEAD_SIZE : (tile + 1) * HEAD_SIZE].astype(jnp.float32)
                total = total + piece * piece
            squares[0, at, :] = total

    square_copies = [
        pltpu.make_async_remote_copy(
            src_ref=squares.at[0, pl.ds(side * mid, mid), :],
            dst_ref=squares.at[1, pl.ds(side * mid, mid), :],
            send_sem=square_sems.at[side, 0],
            recv_sem=square_sems.at[side, 1],
            device_id=partner,
            device_id_type=MESH,
        )
        for side in range(2)
    ]
    for copy in small:
        copy.wait()
    lane64 = lax.broadcasted_iota(jnp.int32, (slots, slots), 1)
    eye64 = lax.broadcasted_iota(jnp.int32, (slots, slots), 0) == lane64
    parent_columns = []
    for p in range(requests):
        row = jnp.broadcast_to(parents_ref[p : p + 1, :].astype(jnp.float32), (slots, slots))
        parent_columns.append(
            jnp.sum(jnp.where(eye64, row, 0.0), axis=1, keepdims=True) + float(p * slots)
        )
    parent_column = jnp.concatenate(parent_columns, axis=0).astype(jnp.int32)
    row_at = lax.broadcasted_iota(jnp.int32, (rows, rows), 0)
    lane_at = lax.broadcasted_iota(jnp.int32, (rows, rows), 1)
    linked = jnp.where((lane_at == parent_column) | (row_at == lane_at), 1.0, 0.0).astype(
        jnp.bfloat16
    )
    doublings = max(1, (slots - 1).bit_length())
    early = doublings // 3
    for doubling in range(early):
        linked = jnp.minimum(
            jnp.dot(linked, linked, preferred_element_type=jnp.float32), 1.0
        ).astype(jnp.bfloat16)
    reach[...] = linked
    square_up(0)
    pl.semaphore_wait(barrier, device_count - 1)
    square_copies[0].start()
    square_up(1)
    square_copies[1].start()

    linked = reach[...]
    for doubling in range(doublings - early):
        linked = jnp.minimum(
            jnp.dot(linked, linked, preferred_element_type=jnp.float32), 1.0
        ).astype(jnp.bfloat16)
    row_id = lax.broadcasted_iota(jnp.int32, (rows, HEAD_SIZE), 0)
    lane_id = lax.broadcasted_iota(jnp.int32, (rows, HEAD_SIZE), 1)
    length_at = jnp.zeros((rows, HEAD_SIZE), jnp.float32)
    end_at = jnp.zeros((rows, HEAD_SIZE), jnp.int32)
    for p in range(requests):
        here = row_id // slots == p
        length_at = jnp.where(here, lengths_ref[p].astype(jnp.float32), length_at)
        end_at = jnp.where(here, counts_ref[p] + p * slots, end_at)
    live[...] = jnp.where(row_id < end_at, 1.0, 0.0)
    for side in sides:
        slot_at = lax.broadcasted_iota(jnp.int32, (mid, mid), 1) + side.start
        within = jnp.where(slot_at < end_at[side], linked[side, side].astype(jnp.float32), 0.0)
        caps[side, :] = jnp.where(within > 0.5, keep_score, masked_score)
    gain = gain_ref[...].astype(jnp.float32).reshape(1, half)

    for at in range(half_chunks):
        wo_load(at).start()

    square_copies[0].wait()
    for load in loads[:3]:
        load.wait()

    def norm_copy(block):
        at = pl.ds(block * norm_rows, norm_rows)
        return pltpu.make_async_remote_copy(
            src_ref=normed.at[0, at, :],
            dst_ref=normed.at[1, at, :],
            send_sem=norm_send.at[block],
            recv_sem=norm_recv.at[block],
            device_id=partner,
            device_id_type=MESH,
        )

    def normalise(block):
        for first in range(block * norm_rows, (block + 1) * norm_rows, step_rows):
            at = slice(first, first + step_rows)
            square = jnp.sum(squares[0, at, :] + squares[1, at, :], axis=1, keepdims=True)
            scale = lax.rsqrt(square / (2.0 * half) + rms_epsilon)
            normed[0, at, :] = (hid[at, :].astype(jnp.float32) * scale * gain).astype(
                jnp.bfloat16
            )
        norm_copy(block).start()

    def rotate(block, at):
        return (
            block * cosine[at, :] + pltpu.roll(block, HEAD_SIZE // 2, 1) * sine[at, :]
        ).astype(jnp.bfloat16)

    chunks = q_width // Q_COLS + 2

    def weight(part, n):
        if n < q_width // Q_COLS:
            return wq[part, :, n * Q_COLS : (n + 1) * Q_COLS]
        return (wk if n == q_width // Q_COLS else wv)[part]

    def first_pass(n, at):
        projected[n, at, :] = jnp.dot(
            normed[0, at, :], weight(0, n), preferred_element_type=jnp.float32
        )

    def second_pass(n, at):
        product = projected[n, at, :] + jnp.dot(
            normed[1, at, :], weight(1, n), preferred_element_type=jnp.float32
        )
        if n == chunks - 1:
            v_new[at, :] = product.astype(jnp.bfloat16)
            return
        for h in range(product.shape[1] // HEAD_SIZE):
            turned = rotate(product[:, h * HEAD_SIZE : (h + 1) * HEAD_SIZE], at)
            if n == chunks - 2:
                k_rot[at, h * HEAD_SIZE : (h + 1) * HEAD_SIZE] = turned
            else:
                first = n * Q_COLS + h * HEAD_SIZE
                q_rot[at, first : first + HEAD_SIZE] = turned

    half_blocks = norm_blocks // 2
    for block in range(half_blocks):
        normalise(block)
    square_copies[1].wait()
    for n in range(chunks):
        first_pass(n, sides[0])
        if n < half_blocks:
            normalise(half_blocks + n)
    depth = jnp.sum(linked.astype(jnp.float32), axis=1, keepdims=True) - 1.0
    positions = length_at + depth
    low_half = lane_id[0:mid] < HEAD_SIZE // 2
    angles = jnp.where(low_half, positions[0:mid], positions[mid:rows]) * freqs_ref[...]
    for table, value in ((cosine, jnp.cos(angles)), (sine, jnp.sin(angles))):
        turned = pltpu.roll(value, HEAD_SIZE // 2, 1)
        sign = 1.0 if table is cosine else -1.0
        table[sides[0], :] = jnp.where(low_half, sign * value, turned)
        table[sides[1], :] = jnp.where(low_half, sign * turned, value)
    for n in range(chunks):
        first_pass(n, sides[1])

    for load in loads[3:]:
        load.wait()
    for at in range(half_chunks, 2 * half_chunks):
        wo_load(at).start()

    for block in range(half_blocks):
        norm_copy(block).wait()
    key_chunk = q_width // Q_COLS
    order = [key_chunk, key_chunk + 1] + list(range(key_chunk))
    for n in order:
        second_pass(n, sides[0])

    factor = math.log2(math.e) / math.sqrt(HEAD_SIZE)
    contract_last = (((1,), (1,)), ((), ()))
    cache_lane = lax.broadcasted_iota(jnp.int32, (1, cache_len), 1)
    steps = [(p, g) for p in range(requests) for g in range(key_heads)]

    def places(i):
        p, g = steps[i]
        pair = slice(p * slots // mid * mid, p * slots // mid * mid + mid)
        return p, g, slice(p * slots, (p + 1) * slots), pair, slice(g * HEAD_SIZE, (g + 1) * HEAD_SIZE)

    def score(i):
        p, g, at, pair, columns = places(i)
        pieces = []
        for h in range(group):
            head = g * group + h
            pieces.append(q_rot[at, head * HEAD_SIZE : (head + 1) * HEAD_SIZE])
        queries = jnp.concatenate(pieces, axis=0)
        cache_scores[i] = lax.dot_general(
            queries, ck[p, :, columns], contract_last, preferred_element_type=jnp.float32
        )
        slot_scores[i] = lax.dot_general(
            queries, k_rot[pair, columns], contract_last, preferred_element_type=jnp.float32
        )

    def soften(i):
        p, g, at, pair, columns = places(i)
        cache_cap = jnp.where(cache_lane < lengths_ref[p], keep_score, masked_score)
        slot_cap = jnp.concatenate([caps[at, :]] * group, axis=0)
        tiles = [
            jnp.minimum(cache_scores[i, :, t : t + HEAD_SIZE], cache_cap[:, t : t + HEAD_SIZE])
            for t in range(0, cache_len, HEAD_SIZE)
        ]
        tiles.append(jnp.minimum(slot_scores[i], slot_cap))
        highest = functools.reduce(jnp.maximum, tiles)
        highest = jnp.max(highest, axis=1, keepdims=True)
        tiles = [jnp.exp2((tile - highest) * factor) for tile in tiles]
        total = jnp.sum(functools.reduce(jnp.add, tiles), axis=1, keepdims=True)
        totals[i] = jnp.broadcast_to(total, totals.shape[1:])
        for t, tile in enumerate(tiles[:-1]):
            cache_probs[i, :, t * HEAD_SIZE : (t + 1) * HEAD_SIZE] = tile.astype(jnp.bfloat16)
        slot_probs[i] = tiles[-1].astype(jnp.bfloat16)

    def collect(i):
        p, g, at, pair, columns = places(i)
        weighted = jnp.dot(
            cache_probs[i], cv[p, :, columns], preferred_element_type=jnp.float32
        ) + jnp.dot(slot_probs[i], v_new[pair, columns], preferred_element_type=jnp.float32)
        result = (weighted / totals[i]).astype(jnp.bfloat16)
        for h in range(group):
            head = g * group + h
            att[at, head * HEAD_SIZE : (head + 1) * HEAD_SIZE] = result[
                h * slots : (h + 1) * slots
            ]

    def part_copy(c, side):
        return pltpu.make_async_remote_copy(
            src_ref=part_send.at[c, sides[side], :],
            dst_ref=part_recv.at[c, sides[side], :],
            send_sem=part_send_sems.at[c, side],
            recv_sem=part_recv_sems.at[c, side],
            device_id=partner,
            device_id_type=MESH,
        )

    def send_part(c, side):
        at = sides[side]
        part_send[c, at, :] = jnp.dot(
            att[at, :], wo[c], preferred_element_type=jnp.float32
        ).astype(jnp.bfloat16)

    def own_product(c, side):
        at = sides[side]
        own_part[c, at, :] = jnp.dot(
            att[at, :], wo[half_chunks + c], preferred_element_type=jnp.float32
        )

    def add_up(c, side):
        at = sides[side]
        features = slice(c * O_COLS, (c + 1) * O_COLS)
        summed = (
            hid[at, features].astype(jnp.float32)
            + own_part[c, at, :]
            + part_recv[c, at, :].astype(jnp.float32)
        )
        head = head_ref[features].astype(jnp.float32).reshape(1, O_COLS)
        scored = jnp.zeros((mid, HEAD_SIZE), jnp.float32)
        for part in range(O_COLS // HEAD_SIZE):
            columns = slice(part * HEAD_SIZE, (part + 1) * HEAD_SIZE)
            kept = jnp.where(live[at, :] > 0.5, summed[:, columns], 0.0).astype(jnp.bfloat16)
            out_ref[c, at, columns] = kept
            scored = scored + kept.astype(jnp.float32) * head[:, columns]
        score_acc[at, :] = scored if c == 0 else score_acc[at, :] + scored

    for block in range(half_blocks, norm_blocks):
        norm_copy(block).wait()
    load_ck.wait()
    load_cv.wait()
    score(0)
    score(1)
    middle = len(steps) // 2
    pending = list(order)
    for i in range(len(steps)):
        if i == middle:
            for c in range(half_chunks):
                wo_load(c).wait()
        soften(i)
        for n in pending[: -(-len(order) // max(middle - 1, 1))]:
            pending.remove(n)
            second_pass(n, sides[1])
        if i + 2 < len(steps):
            score(i + 2)
        if i > 0:
            collect(i - 1)
        if i == middle:
            for c in range(half_chunks):
                send_part(c, 0)
            for c in range(half_chunks):
                part_copy(c, 0).start()
    collect(len(steps) - 1)
    for first in range(0, half_chunks, 2):
        for c in range(first, first + 2):
            send_part(c, 1)
        for c in range(first, first + 2):
            part_copy(c, 1).start()
    for c in range(half_chunks):
        wo_load(half_chunks + c).wait()
    for c in range(half_chunks):
        own_product(c, 0)
    for c in range(half_chunks):
        part_copy(c, 0).wait()
    for c in range(half_chunks):
        own_product(c, 1)
        add_up(c, 0)
    for c in range(half_chunks):
        part_copy(c, 1).wait()
    for c in range(half_chunks):
        add_up(c, 1)

    per_line = HEAD_SIZE // slots
    line_row = lax.broadcasted_iota(jnp.int32, (slots, HEAD_SIZE), 0)
    line_lane = lax.broadcasted_iota(jnp.int32, (slots, HEAD_SIZE), 1)
    lines = []
    for first in range(0, requests, per_line):
        line = jnp.zeros((slots, HEAD_SIZE), jnp.float32)
        for p in range(first, first + per_line):
            column = jnp.sum(score_acc[p * slots : (p + 1) * slots, :], axis=1, keepdims=True)
            line = jnp.where(line_lane - (p - first) * slots == line_row, column, line)
        lines.append(jnp.sum(line, axis=0, keepdims=True))
    scores = jnp.concatenate(lines, axis=0)
    mine[...] = scores
    gathered[flat] = scores

    @pl.loop(0, device_count - 1, unroll=8)
    def _(step):
        pltpu.make_async_remote_copy(
            src_ref=mine,
            dst_ref=gathered.at[flat],
            send_sem=all_send,
            recv_sem=all_recv,
            device_id=target_of(step),
            device_id_type=MESH,
        ).start()

    per_request = accept_ref.shape[1]
    picks = requests * per_request * 2
    pick_row = lax.broadcasted_iota(jnp.int32, (picks, rows), 0)
    pick_lane = lax.broadcasted_iota(jnp.int32, (picks, rows), 1)
    wanted = jnp.zeros((picks, rows), jnp.int32)
    for p in range(requests):
        for a in range(per_request):
            wanted = jnp.where(
                pick_row // 2 == p * per_request + a, accept_ref[p, a] + p * slots, wanted
            )
    chosen = pick_lane == wanted
    odd = lax.rem(pick_row, 2) == 1
    pick_keys = jnp.where(chosen & ~odd, 1.0, 0.0).astype(jnp.bfloat16)
    pick_values = jnp.where(chosen & odd, 1.0, 0.0).astype(jnp.bfloat16)
    picked_rows = jnp.dot(
        pick_keys, k_rot[...], preferred_element_type=jnp.float32
    ) + jnp.dot(pick_values, v_new[...], preferred_element_type=jnp.float32)
    rows_ref[...] = picked_rows.reshape(rows_ref.shape).astype(jnp.bfloat16)

    everything = gathered.at[pl.ds(0, device_count - 1)]
    whole = pltpu.make_async_remote_copy(
        src_ref=everything,
        dst_ref=everything,
        send_sem=all_send,
        recv_sem=all_recv,
        device_id=partner,
        device_id_type=MESH,
    )
    whole.wait_send()
    whole.wait_recv()

    shape = (device_count, requests // per_line, HEAD_SIZE)
    source = lax.broadcasted_iota(jnp.int32, shape, 0) // narrow_count
    line_at = lax.broadcasted_iota(jnp.int32, shape, 1)
    place = lax.broadcasted_iota(jnp.int32, shape, 2) // slots
    request_at = source * requests + line_at * per_line + place
    values = gathered[...]
    for r in range(requests):
        picked = jnp.sum(jnp.where(request_at == order_ref[r], values, 0.0), axis=0)
        picked = jnp.sum(picked, axis=0, keepdims=True)
        total = picked[:, :slots]
        for part in range(1, per_line):
            total = total + picked[:, part * slots : (part + 1) * slots]
        verify_ref[r : r + 1, :] = total


def body(
    hidden_in,
    norm_gain,
    w_query,
    key_weight,
    value_weight,
    w_out,
    cached_key_rows,
    cached_value_rows,
    lengths,
    counts,
    parents,
    accept,
    order_map,
    accept_head,
):
    wide_count = lax.axis_size("wide")
    narrow_count = lax.axis_size("narrow")
    device_count = wide_count * narrow_count
    rows, half = hidden_in.shape
    requests, slots = parents.shape
    per_request = accept.shape[1]
    query_width = w_query.shape[1]
    key_width = key_weight.shape[1]
    norm_blocks = 2
    key_heads = key_width // HEAD_SIZE
    steps = requests * key_heads
    grouped = query_width // key_width * slots
    cache_len = cached_key_rows.shape[1]
    half_chunks = half // O_COLS
    q_chunks = query_width // Q_COLS
    exponents = np.arange(HEAD_SIZE) % (HEAD_SIZE // 2) * 2.0 / HEAD_SIZE
    freqs = jnp.asarray((10000.0**-exponents)[None, :].astype(np.float32))
    hbm_spec = pl.BlockSpec(memory_space=pltpu.HBM)
    vmem_spec = pl.BlockSpec(memory_space=pltpu.VMEM)
    bf16, f32 = jnp.bfloat16, jnp.float32
    hidden, picked_rows, scores = pl.pallas_call(
        functools.partial(layer_kernel, wide_count, narrow_count),
        out_shape=(
            jax.ShapeDtypeStruct((half_chunks, rows, O_COLS), bf16),
            jax.ShapeDtypeStruct((requests, per_request, 2, key_width), bf16),
            jax.ShapeDtypeStruct((requests, slots), f32),
        ),
        in_specs=[hbm_spec] * 15,
        out_specs=(vmem_spec, vmem_spec, vmem_spec),
        scratch_shapes=[
            pltpu.VMEM(norm_gain.shape, bf16),
            pltpu.VMEM(accept_head.shape, bf16),
            pltpu.VMEM(freqs.shape, f32),
            pltpu.VMEM(parents.shape, parents.dtype),
            pltpu.SMEM(lengths.shape, lengths.dtype),
            pltpu.SMEM(counts.shape, counts.dtype),
            pltpu.SMEM(accept.shape, accept.dtype),
            pltpu.SMEM(order_map.shape, order_map.dtype),
            pltpu.VMEM((rows, half), bf16),
            pltpu.VMEM((2, rows, half), bf16),
            pltpu.VMEM((2, rows, HEAD_SIZE), f32),
            pltpu.VMEM((2, half, query_width), bf16),
            pltpu.VMEM((2, half, key_width), bf16),
            pltpu.VMEM((2, half, key_width), bf16),
            pltpu.VMEM((2 * half_chunks, query_width, O_COLS), bf16),
            pltpu.VMEM(cached_key_rows.shape, bf16),
            pltpu.VMEM(cached_value_rows.shape, bf16),
            pltpu.VMEM((q_chunks + 2, rows, Q_COLS), f32),
            pltpu.VMEM((half_chunks, rows, O_COLS), f32),
            pltpu.VMEM((rows, rows), bf16),
            pltpu.VMEM((rows, rows // 2), f32),
            pltpu.VMEM((steps, grouped, cache_len), f32),
            pltpu.VMEM((steps, grouped, rows // 2), f32),
            pltpu.VMEM((steps, grouped, cache_len), bf16),
            pltpu.VMEM((steps, grouped, rows // 2), bf16),
            pltpu.VMEM((steps, grouped, HEAD_SIZE), f32),
            pltpu.VMEM((rows, HEAD_SIZE), f32),
            pltpu.VMEM((rows, HEAD_SIZE), f32),
            pltpu.VMEM((rows, HEAD_SIZE), f32),
            pltpu.VMEM((rows, query_width), bf16),
            pltpu.VMEM((rows, key_width), bf16),
            pltpu.VMEM((rows, key_width), bf16),
            pltpu.VMEM((rows, query_width), bf16),
            pltpu.VMEM((half_chunks, rows, O_COLS), bf16),
            pltpu.VMEM((half_chunks, rows, O_COLS), bf16),
            pltpu.VMEM((rows, HEAD_SIZE), f32),
            pltpu.VMEM((requests * slots // HEAD_SIZE, HEAD_SIZE), f32),
            pltpu.VMEM((device_count, requests * slots // HEAD_SIZE, HEAD_SIZE), f32),
            pltpu.SemaphoreType.DMA((8,)),
            pltpu.SemaphoreType.DMA((10,)),
            pltpu.SemaphoreType.DMA((2 * half_chunks,)),
            pltpu.SemaphoreType.DMA((2, 2)),
            pltpu.SemaphoreType.DMA((norm_blocks,)),
            pltpu.SemaphoreType.DMA((norm_blocks,)),
            pltpu.SemaphoreType.DMA((half_chunks, 2)),
            pltpu.SemaphoreType.DMA((half_chunks, 2)),
            pltpu.SemaphoreType.DMA,
            pltpu.SemaphoreType.DMA,
        ],
        compiler_params=pltpu.CompilerParams(
            collective_id=0, has_side_effects=True, vmem_limit_bytes=50 * 2**20
        ),
    )(
        *(
            pltpu.with_memory_space_constraint(operand, pltpu.HBM)
            for operand in (
                hidden_in,
                norm_gain,
                accept_head,
                freqs,
                w_query,
                key_weight,
                value_weight,
                w_out,
                cached_key_rows,
                cached_value_rows,
                parents,
                lengths,
                counts,
                accept,
                order_map,
            )
        )
    )
    return pl.pallas_call(
        finish_kernel,
        out_shape=(
            jax.ShapeDtypeStruct((rows, half), bf16),
            jax.ShapeDtypeStruct((requests, per_request, 2, key_width), bf16),
            jax.ShapeDtypeStruct((requests, slots), f32),
        ),
        in_specs=[vmem_spec, vmem_spec, vmem_spec],
        out_specs=(hbm_spec, hbm_spec, hbm_spec),
        scratch_shapes=[pltpu.SemaphoreType.DMA((half_chunks + 2,))],
        compiler_params=pltpu.CompilerParams(vmem_limit_bytes=8 * 2**20),
    )(hidden, picked_rows, scores)


def solution(mesh):
    placed = (
        P("wide", "narrow"),
        P("narrow"),
        P(None, "narrow"),
        P(None, "narrow"),
        P(None, "narrow"),
        P("narrow", None),
        P("wide", None, "narrow"),
        P("wide", None, "narrow"),
        P("wide"),
        P("wide"),
        P("wide", None),
        P("wide", None),
        P("wide"),
        P("narrow"),
    )
    return jax.shard_map(
        body,
        mesh=mesh,
        in_specs=placed,
        out_specs=(P("wide", "narrow"), P("wide", None, None, "narrow"), P("wide", None)),
        check_vma=False,
    )
```
